32 devices in a mesh: node: 4 (over y, x), local: 4 (over z), rep: 2 (over core).
Axes of the slice: x: 2, y: 2, z: 4, core: 2. Of those that a mesh axis runs over, the one named last changes fastest.
Arguments:
- grad_out: bfloat16 [256, 4096], P(('node', 'local', 'rep')), may hold values from -0.59765625 to 0.59765625
- expert_ids: int32 [256, 4], P(('node', 'local', 'rep')), may hold values from 0 to 15, as said below
- route_weights: bfloat16 [256, 4], P(('node', 'local', 'rep')), may hold values from 0.19921875 to 2
- gate_pre: bfloat16 [128, 16384], P('rep', ('node', 'local')), may hold values from -6 to 6
- up_pre: bfloat16 [128, 16384], P('rep', ('node', 'local')), may hold values from -6 to 6
- w_down_t: bfloat16 [4096, 16384], P(None, ('node', 'local')), may hold values from -0.1875 to 0.1875
Outputs:
- grad_gate_pre: bfloat16 [128, 16384], P('rep', ('node', 'local'))
- grad_up_pre: bfloat16 [128, 16384], P('rep', ('node', 'local'))
- grad_down_t: bfloat16 [4096, 16384], P('rep', ('node', 'local'))
- grad_route: bfloat16 [256, 16], P(('local', 'rep'), 'node')
The draws below stay inside these ranges and needn't reach their ends.
Inputs may be any that keep to these rules, and one draw needn't show every extreme that they name: `expert_ids`: each token names 4 different experts: 2 in each of 2 different groups (group of e = e // 4). In every cohort each group is named by exactly 16 tokens, and within it exactly 1 expert are named 16 times, 2 experts 8 times and the others never. In every group one expert is named 16 times by every cohort.
All inputs are finite; a program needn't handle non-finite values.
Results may differ from the reference program's by a relative error of at most 0.013.
Values may be sent and summed in bfloat16 or wider, within the bound.
A program may use at most 64 MiB of HBM per device.

```python
import math
from functools import partial
import jax
import jax.numpy as jnp
from jax import lax

D = 4096
H = 1024
PER_GROUP = 2
TOK_DEV = 8
GROUPS_TOK = 2
TOP = 4
OWNERS = 1
HS = 1024
EXP_GROUP = 4
EXPERTS = 16
TOKENS = 256
COHORT = 32
HALF = 8
CAP = 16
FULL = 1
SLOTS = 64
N_NODE = 4
N_LOCAL = 4
N_REP = 2


def group_ranking(group_key, hot_expert):
    scores_int = jax.random.permutation(group_key, EXP_GROUP).astype(jnp.int32)
    scores_int = jnp.where(jnp.arange(EXP_GROUP, dtype=jnp.int32) == hot_expert, -1, scores_int)
    return jnp.argsort(scores_int, stable=True).astype(jnp.int32)


def cohort_routes(hot_experts, cohort_key):
    key_list = jax.random.split(cohort_key, 3)
    group_order = jax.random.permutation(key_list[0], N_NODE).astype(jnp.int32)
    token_order = jax.random.permutation(key_list[1], COHORT).astype(jnp.int32)
    expert_keys = jax.random.split(key_list[2], N_NODE)
    ranking = jax.vmap(group_ranking)(expert_keys, hot_experts)
    position = jnp.arange(COHORT, dtype=jnp.int32)
    choice_col = jnp.arange(GROUPS_TOK, dtype=jnp.int32)
    group_rank = (GROUPS_TOK * position[:, None] + choice_col[None, :]) % N_NODE
    chooses = jnp.sum((group_rank[:, :, None] == jnp.arange(N_NODE, dtype=jnp.int32)[None, None, :]).astype(jnp.int32), axis=1)
    before = jnp.cumsum(chooses, axis=0) - chooses
    token_rank = jnp.take_along_axis(before, group_rank, axis=1)
    pick_col = jnp.arange(PER_GROUP, dtype=jnp.int32)
    pick_index = token_rank[:, :, None] + TOK_DEV * GROUPS_TOK * pick_col[None, None, :]
    expert_rank = jnp.where(pick_index < FULL * CAP, pick_index // CAP, FULL + (pick_index - FULL * CAP) // HALF)
    group_id = group_order[group_rank]
    chosen = ranking[group_id[:, :, None], expert_rank]
    expert_id = group_id[:, :, None] * EXP_GROUP + chosen
    virtual = expert_id.reshape(COHORT, TOP)
    return virtual[jnp.argsort(token_order, stable=True)]


def draw_expert_ids(key, part):
    key_pair = jax.random.split(jax.random.fold_in(key, 11))
    hot_experts = jax.random.randint(key_pair[0], (N_NODE,), 0, EXP_GROUP).astype(jnp.int32)
    cohort_keys = jax.random.split(key_pair[1], N_LOCAL * N_REP)
    routes = jax.vmap(partial(cohort_routes, hot_experts))(cohort_keys)
    routes = routes.reshape(N_LOCAL, N_REP, N_NODE, TOK_DEV, TOP).transpose(2, 0, 1, 3, 4)
    return routes.reshape(TOKENS, TOP).astype(jnp.int32)


def steps_of(own_key, dims, shards, smallest, largest):
    factor_of, own = 1.0, jax.random.fold_in(own_key, 6)
    for dim, shards_of in shards:
        draws = jnp.exp(jax.random.uniform(jax.random.fold_in(own, dim), (shards_of,), jnp.float32, smallest / len(shards), largest / len(shards)))
        factor_of = factor_of * jnp.repeat(draws, dims[dim] // shards_of).reshape([-1 if axis == dim else 1 for axis in range(len(dims))])
    return factor_of


def scatter_about(key, dims, spread, reach, pieces=(), kind=jnp.bfloat16):
    values = jax.random.normal(key, dims, jnp.float32) * spread
    if len(pieces) > 0:
        values = steps_of(key, dims, pieces, -0.22, 0.18) * values
    return jnp.clip(values, min=-reach, max=reach).astype(kind)


def setup_inputs(seed: int = 0) -> dict:
    key_of = jax.random.split(jax.random.key(seed), 7)
    grad_out = scatter_about(key_of[0], (TOKENS, D), 0.1, 0.59765625, ((0, 32),))
    expert_ids = draw_expert_ids(jax.random.fold_in(key_of[6], 71), 0)
    route_weights = jnp.clip(jnp.exp(math.log(2.0) - 2.306499 * jax.random.uniform(key_of[2], (TOKENS, TOP), jnp.float32) ** steps_of(key_of[2], (TOKENS, TOP), ((0, 32),), -0.2, 0.2)), 0.19921875, 2.0).astype(jnp.bfloat16)
    gate_pre = scatter_about(key_of[3], (N_REP * SLOTS, EXPERTS * H), 1.0, 6.0, ((0, 2), (1, 16)))
    up_pre = scatter_about(key_of[4], (N_REP * SLOTS, EXPERTS * H), 1.0, 6.0, ((0, 2), (1, 16)))
    w_down_t = scatter_about(key_of[5], (D, EXPERTS * H), H ** -0.5, 0.1875, ((1, 16),))
    return dict(grad_out=grad_out, expert_ids=expert_ids, route_weights=route_weights, gate_pre=gate_pre, up_pre=up_pre, w_down_t=w_down_t)


def to_cohorts(array):
    tail = array.shape[1]
    shaped = array.reshape(N_NODE, N_LOCAL, N_REP, TOK_DEV, tail)
    return shaped.transpose(1, 2, 0, 3, 4).reshape(N_LOCAL, N_REP, COHORT, tail)


def reference(grad_out, expert_ids, route_weights, gate_pre, up_pre, w_down_t):
    ids_cohort = to_cohorts(expert_ids)
    weights_cohort = to_cohorts(route_weights)
    grad_cohort = to_cohorts(grad_out)
    expert_range = jnp.arange(EXPERTS, dtype=jnp.int32)
    route_hits = (ids_cohort[..., None] == expert_range).astype(jnp.int32)
    per_expert = jnp.sum(route_hits, axis=3)
    earlier = jnp.cumsum(per_expert, axis=2) - per_expert
    slot_index = jnp.sum(route_hits * earlier[:, :, :, None, :], axis=4).astype(jnp.int32)
    local_index = jnp.arange(N_LOCAL, dtype=jnp.int32)[:, None, None, None]
    replica_index = jnp.arange(N_REP, dtype=jnp.int32)[None, :, None, None]
    flat_index = (((ids_cohort * N_REP + replica_index) * N_LOCAL + local_index) * CAP + slot_index).astype(jnp.int32)
    flat_index = flat_index.reshape(-1)
    total_rows = EXPERTS * N_REP * SLOTS
    source_rows = jnp.broadcast_to(grad_cohort[:, :, :, None, :], (N_LOCAL, N_REP, COHORT, TOP, D)).reshape(-1, D)
    packed = jnp.zeros((total_rows, D), jnp.bfloat16).at[flat_index].set(source_rows)
    packed = packed.reshape(EXPERTS, N_REP * SLOTS, D)
    packed_weights = jnp.zeros((total_rows,), jnp.float32).at[flat_index].set(weights_cohort.reshape(-1).astype(jnp.float32))
    packed_weights = packed_weights.reshape(EXPERTS, N_REP * SLOTS)

    def one_expert(expert_index):
        cotangent = lax.dynamic_index_in_dim(packed, expert_index, 0, keepdims=False)
        weight = lax.dynamic_index_in_dim(packed_weights, expert_index, 0, keepdims=False)[:, None]
        column_start = expert_index * H
        gate_value = lax.dynamic_slice_in_dim(gate_pre, column_start, H, 1).astype(jnp.float32)
        up_value = lax.dynamic_slice_in_dim(up_pre, column_start, H, 1).astype(jnp.float32)
        down_cols = lax.dynamic_slice_in_dim(w_down_t, column_start, H, 1)
        backward = jnp.dot(cotangent, down_cols, preferred_element_type=jnp.float32)
        sigmoid_gate = jax.nn.sigmoid(gate_value)
        activated = gate_value * sigmoid_gate
        hidden = activated * up_value
        shares = jnp.sum((hidden * backward).reshape(N_REP * SLOTS, OWNERS, HS), axis=2).astype(jnp.bfloat16)
        score_value = jnp.sum(shares.astype(jnp.float32), axis=1).astype(jnp.bfloat16)
        scaled = weight * backward
        grad_gate = (scaled * up_value * sigmoid_gate * (1.0 + gate_value * (1.0 - sigmoid_gate))).astype(jnp.bfloat16)
        grad_up = (scaled * activated).astype(jnp.bfloat16)
        weighted = (weight * hidden).astype(jnp.bfloat16)
        total = jnp.zeros((D, H), jnp.float32)
        for replica in range(N_REP):
            term = lax.dot_general(cotangent[replica * SLOTS:(replica + 1) * SLOTS], weighted[replica * SLOTS:(replica + 1) * SLOTS], (((0,), (0,)), ((), ())), preferred_element_type=jnp.float32)
            total = total + term.astype(jnp.bfloat16).astype(jnp.float32)
        return score_value, grad_gate, grad_up, total.astype(jnp.bfloat16)

    score_all, gate_all, up_all, down_all = lax.map(one_expert, jnp.arange(EXPERTS, dtype=jnp.int32))
    grad_gate_pre = gate_all.transpose(1, 0, 2).reshape(N_REP * SLOTS, EXPERTS * H)
    grad_up_pre = up_all.transpose(1, 0, 2).reshape(N_REP * SLOTS, EXPERTS * H)
    grad_down_t = down_all.transpose(1, 0, 2).reshape(D, EXPERTS * H)
    route_values = score_all.reshape(-1)[flat_index].reshape(N_LOCAL, N_REP, COHORT, TOP).astype(jnp.float32)
    dense_grad = jnp.sum(route_hits.astype(jnp.float32) * route_values[..., None], axis=3)
    grad_route = dense_grad.reshape(N_LOCAL * N_REP * COHORT, EXPERTS).astype(jnp.bfloat16)
    return grad_gate_pre, grad_up_pre, grad_down_t, grad_route
```

```python
import functools
import jax
import jax.numpy as jnp
from jax import lax
from jax.experimental import pallas as pl
from jax.experimental.pallas import tpu as pltpu
from jax.sharding import PartitionSpec as P

H = 1024
PER_GROUP = 2
PAIRS = (("near", 4), ("far", 4), ("near", 4), ("far", 4))
TILE = 256
REACH = 2
MESH = pl.DeviceIdType.MESH
F32 = jnp.float32
BF16 = jnp.bfloat16
KERNEL_PARAMS = dict(vmem_limit_bytes=40 * 1024 * 1024)


def contract_rows(left, right):
    return lax.dot_general(left, right, (((0,), (0,)), ((), ())), preferred_element_type=F32)


def one_hot(member, row, height):
    places = lax.broadcasted_iota(jnp.int32, (height, member.shape[1]), 0).astype(F32)
    return jnp.where((member > 0) & (row == places), 1.0, 0.0)


def earlier_counts(rows, block):
    count = rows.shape[1]
    above = lax.broadcasted_iota(jnp.int32, (count, count), 0)
    col = lax.broadcasted_iota(jnp.int32, (count, count), 1)
    strict = jnp.where((above < col) & (above // block == col // block), 1.0, 0.0).astype(BF16)
    return jnp.dot(rows.astype(BF16), strict, preferred_element_type=F32)


def stacked(rows):
    lines = lax.broadcasted_iota(jnp.int32, (8, rows[0].shape[1]), 0)
    out = jnp.zeros(lines.shape, F32)
    for place, row in enumerate(rows):
        out = jnp.where(lines == place, row, out)
    return out


def column_pairs(half):
    parts = sum(share for _, share in PAIRS)
    pairs, taken, at = [], {"near": 0, "far": 0}, 0
    for way, share in PAIRS:
        size = half * share // parts
        pairs.append((way, at, size, taken[way]))
        taken[way] += 2 * size
        at += size
    return pairs, taken["near"], taken["far"]


def routed_kernel(
    dims, ids_ref, rw_ref, grad_ref, gate_ref, up_ref, w_ref,
    ggate_out, gup_out, down_out, route_out,
    cot_out, wtd_out, ids_buf, rw_buf, meta, cohort_meta, nraw, gath, zraw, peer_cot, w_buf, gate_up,
    acc, hidden_buf, gate_factor, up_factor, share_buf, back_buf,
    own_sem, load_sem, w_sem,
    meta_send, meta_recv, raw_send, nraw_recv, zraw_send, zraw_recv, plane_send, plane_recv,
    pack_send, pack_recv, relay_send, cmeta_send, cmeta_recv,
    wtd_send, wtd_recv, cot_send, cot_recv, share_send, share_recv,
):
    nodes, locals_, tok, top, width, hs, group_tok, owners = dims
    cohort = nodes * tok
    exp_group = locals_ // owners
    slots = gate_ref.shape[0]
    capacity = slots // locals_
    half = width // 2
    pairs, near_width, far_width = column_pairs(half)
    near = [p for p, pair in enumerate(pairs) if pair[0] == "near"]
    far = [p for p, pair in enumerate(pairs) if pair[0] == "far"]
    me_n, me_l, me_r = lax.axis_index("node"), lax.axis_index("local"), lax.axis_index("rep")
    peer = {"rep": 1 - me_r}

    def node_at(k):
        return {"node": lax.rem(me_n + k, nodes)}

    def local_at(k):
        return {"local": lax.rem(me_l + k, locals_)}

    def remote(src, dst, send, recv, device):
        return pltpu.make_async_remote_copy(
            src_ref=src, dst_ref=dst, send_sem=send, recv_sem=recv,
            device_id=device, device_id_type=MESH,
        )

    def received(ref, sem):
        remote(ref, ref, sem, sem, peer).wait_recv()

    def sent(ref, sem):
        remote(ref, ref, sem, sem, peer).wait_send()

    barrier = pltpu.get_barrier_semaphore()
    for k in range(1, nodes):
        pl.semaphore_signal(barrier, inc=1, device_id=node_at(k), device_id_type=MESH)
    for k in range(1, locals_):
        pl.semaphore_signal(barrier, inc=1, device_id=local_at(k), device_id_type=MESH)
    pl.semaphore_signal(barrier, inc=1, device_id=peer, device_id_type=MESH)

    def block(p):
        return pl.ds(pairs[p][3], 2 * pairs[p][2])

    def part(p):
        return pl.ds(pairs[p][1], pairs[p][2])

    id_copy = pltpu.make_async_copy(ids_ref, ids_buf, own_sem.at[0])
    rw_copy = pltpu.make_async_copy(rw_ref, rw_buf, own_sem.at[1])
    id_copy.start()
    rw_copy.start()
    for p, (way, at, size, place) in enumerate(pairs):
        for h in range(2):
            here = pl.ds(place + h * size, size)
            target = nraw.at[me_n, :, here] if way == "near" else zraw.at[me_l, me_n, :, here]
            pltpu.make_async_copy(
                grad_ref.at[:, pl.ds(h * half + at, size)], target, own_sem.at[2 if way == "near" else 3]
            ).start()
    pltpu.make_async_copy(gate_ref, gate_up.at[0], load_sem).start()
    pltpu.make_async_copy(up_ref, gate_up.at[1], load_sem).start()
    id_copy.wait()
    rw_copy.wait()
    meta[me_n, 0:top, :] = ids_buf[...].astype(F32)
    meta[me_n, top:2 * top, :] = rw_buf[...].astype(F32)
    own_near, own_far = nraw.at[me_n], zraw.at[me_l, me_n]
    pltpu.make_async_copy(own_near, own_near, own_sem.at[2]).wait()
    pltpu.make_async_copy(own_far, own_far, own_sem.at[3]).wait()
    pl.semaphore_wait(barrier, nodes + locals_ - 1)

    for k in range(1, nodes):
        remote(meta.at[me_n], meta.at[me_n], meta_send, meta_recv, node_at(k)).start()

    def beside(d):
        return [(me_l >= d, me_l - d), (me_l + d < locals_, me_l + d)]

    def far_block(l, n, p):
        return zraw.at[l, n, :, block(p)]

    for i, p in enumerate(near):
        for k in range(1, nodes):
            own = nraw.at[me_n, :, block(p)]
            remote(own, own, raw_send.at[0], nraw_recv.at[i], node_at(k)).start()
    for i, p in enumerate(far):
        for d in range(1, locals_):
            for there, target in beside(d):
                @pl.when(there)
                def _():
                    own = far_block(me_l, me_n, p)
                    remote(own, own, zraw_send, zraw_recv.at[me_l, i], {"local": target}).start()
    for i, p in enumerate(far):
        for k in range(1, nodes):
            own = far_block(me_l, me_n, p)
            remote(own, own, raw_send.at[1], plane_recv.at[i], node_at(k)).start()

    w_at = 0
    w_rows = []
    for p, (way, at, size, place) in enumerate(pairs):
        for h in range(2):
            pltpu.make_async_copy(
                w_ref.at[pl.ds(h * half + at, size), :], w_buf.at[pl.ds(w_at + h * size, size), :], w_sem.at[p]
            ).start()
        w_rows.append(pl.ds(w_at, 2 * size))
        w_at += 2 * size

    pltpu.make_async_copy(gate_up, gate_up, load_sem).wait()
    gate, up = gate_up[0].astype(F32), gate_up[1].astype(F32)
    sig = jax.nn.sigmoid(gate)
    act = gate * sig
    hidden_buf[...] = act * up
    up_factor[...] = act
    gate_factor[...] = up * sig * (1.0 + gate * (1.0 - sig))

    received(meta.at[0:nodes - 1], meta_recv)
    own_meta = jnp.concatenate([meta[n] for n in range(nodes)], axis=1)
    own_ids, own_rw = own_meta[0:top], own_meta[top:2 * top]
    low = (me_n * exp_group).astype(F32)
    named = [jnp.where(own_ids == low + j, 1.0, 0.0) for j in range(exp_group)]
    hits = [jnp.sum(match, axis=0, keepdims=True) for match in named]
    in_group = jnp.where(sum(hits) > 0, 1.0, 0.0)
    before = earlier_counts(stacked(hits + [in_group]), cohort)
    pick = one_hot(in_group, before[exp_group:exp_group + 1], group_tok).astype(BF16)

    def send_pack(i):
        p = near[i]
        received(nraw.at[0:nodes - 1, :, block(p)], nraw_recv.at[i])
        rows = nraw[:, :, block(p)].astype(F32).reshape(cohort, 2 * pairs[p][2]).astype(BF16)
        gath[me_l, :, block(p)] = jnp.dot(pick, rows, preferred_element_type=F32).astype(BF16)
        own = gath.at[me_l, :, block(p)]
        for d in range(min(REACH, locals_ - 1), 0, -1):
            for s, (there, target) in enumerate([(me_l + d < locals_, me_l + d), (me_l >= d, me_l - d)]):
                @pl.when(there)
                def _():
                    remote(own, own, pack_send.at[d - 1, s], pack_recv.at[me_l, i], {"local": target}).start()

    def send_cohort_meta():
        weights = [jnp.sum(match * own_rw, axis=0, keepdims=True) for match in named]
        cohort_meta[me_l] = stacked(weights)[0:exp_group]
        for k in range(1, locals_):
            own = cohort_meta.at[me_l]
            remote(own, own, cmeta_send, cmeta_recv, local_at(k)).start()

    def relays(d):
        return [
            ((me_l >= d) & (me_l + 1 < locals_), me_l - d, me_l + 1),
            ((me_l + d < locals_) & (me_l >= 1), me_l + d, me_l - 1),
        ]

    def relay_pack(i, d):
        for s, (there, source, target) in enumerate(relays(d)):
            @pl.when(there)
            def _():
                pack = gath.at[source, :, block(near[i])]
                received(pack, pack_recv.at[source, i])
                remote(pack, pack, relay_send.at[d - REACH, s], pack_recv.at[source, i], {"local": target}).start()

    def forward(i, d):
        p = far[i]
        for there, source in beside(d):
            @pl.when(there)
            def _():
                piece = far_block(source, me_n, p)
                received(piece, zraw_recv.at[source, i])
                for k in range(1, nodes):
                    remote(piece, piece, plane_send, plane_recv.at[i], node_at(k)).start()

    state = {}

    def prepare():
        received(cohort_meta.at[0:locals_ - 1], cmeta_recv)
        total = locals_ * cohort
        weights = jnp.concatenate([cohort_meta[l] for l in range(locals_)], axis=1)
        mine = lax.broadcasted_iota(jnp.int32, (exp_group, total), 0) == me_l // owners
        row_weight = jnp.sum(jnp.where(mine, weights, 0.0), axis=0, keepdims=True)
        member = jnp.where(row_weight > 0, 1.0, 0.0)
        grouped = jnp.where(jnp.sum(weights, axis=0, keepdims=True) > 0, 1.0, 0.0)
        earlier = earlier_counts(stacked([member, grouped]), cohort)
        which = (lax.broadcasted_iota(jnp.int32, (1, total), 1) // cohort).astype(F32)
        slot_hot = one_hot(member, earlier[0:1] + which * capacity, slots)
        pack_hot = one_hot(grouped, earlier[1:2] + which * group_tok, locals_ * group_tok)
        state["far"] = slot_hot.astype(BF16)
        state["near"] = lax.dot_general(
            slot_hot.astype(BF16), pack_hot.astype(BF16),
            (((1,), (1,)), ((), ())), preferred_element_type=F32,
        ).astype(BF16)
        weight = jnp.sum(slot_hot * row_weight, axis=1, keepdims=True)
        state["weight"] = weight
        wtd_out[0:slots, :] = (weight * hidden_buf[...]).astype(BF16)
        wtd_copy.start()

    wtd_copy = remote(wtd_out.at[0:slots, :], wtd_out.at[slots:2 * slots, :], wtd_send, wtd_recv, peer)

    def cot_copy(p):
        return remote(
            peer_cot.at[:, part(p)], cot_out.at[slots:2 * slots, part(p)], cot_send, cot_recv.at[p], peer,
        )

    def arrived(p):
        if pairs[p][0] == "far":
            received(zraw.at[:, 0:nodes - 1, :, block(p)], plane_recv.at[far.index(p)])
            return
        i = near.index(p)
        for d in range(1, locals_):
            for s, (there, source) in enumerate(beside(d)):
                if REACH <= d < locals_ - 1:
                    there = there & jnp.logical_not(relays(d)[s][0])

                @pl.when(there)
                def _():
                    received(gath.at[source, :, block(p)], pack_recv.at[source, i])

    def finish(p, first):
        way, at, size, place = pairs[p]
        arrived(p)
        if way == "far":
            rows = zraw[:, :, :, block(p)].astype(F32).reshape(locals_ * cohort, 2 * size).astype(BF16)
        else:
            rows = gath[:, :, block(p)].reshape(locals_ * group_tok, 2 * size)
        cot = jnp.dot(state[way], rows, preferred_element_type=F32).astype(BF16)
        for r in range(2):
            @pl.when(me_r == r)
            def _():
                cot_out[0:slots, part(p)] = cot[:, r * size:(r + 1) * size]
                peer_cot[:, part(p)] = cot[:, (1 - r) * size:(2 - r) * size]

        cot_copy(p).start()
        w_part = w_buf.at[w_rows[p], :]
        pltpu.make_async_copy(w_part, w_part, w_sem.at[p]).wait()
        term = jnp.dot(cot, w_buf[w_rows[p], :], preferred_element_type=F32)
        if first:
            acc[...] = term
        else:
            acc[...] += term

    def outer(p, first):
        if first:
            wtd_copy.wait_recv()
        cot_copy(p).wait_recv()
        at, size = pairs[p][1], pairs[p][2]
        for t in range(size // TILE):
            place = pl.ds(at + t * TILE, TILE)
            down_out[place, :] = contract_rows(cot_out[:, place], wtd_out[...]).astype(BF16)

    send_pack(0)
    send_cohort_meta()
    forward(0, 1)
    send_pack(1)
    forward(1, 1)
    forward(0, 2)
    relay_pack(0, 2)
    forward(1, 2)
    forward(0, 3)
    relay_pack(1, 2)
    forward(1, 3)
    prepare()
    order = [near[0], far[0], near[1], far[1]]
    for n, p in enumerate(order):
        finish(p, n == 0)

    back = acc[...]
    shares = jnp.sum(hidden_buf[...] * back, axis=1, keepdims=True)
    share_buf[...] = jnp.broadcast_to(shares, (slots, 128)).astype(BF16).reshape(locals_, capacity, 128)
    for k in range(1, locals_):
        remote(
            share_buf.at[lax.rem(me_l + k, locals_)], back_buf.at[me_l], share_send, share_recv, local_at(k)
        ).start()
    back_buf[me_l] = share_buf[me_l]
    scaled = state["weight"] * back
    ggate_out[...] = (scaled * gate_factor[...]).astype(BF16)
    gup_out[...] = (scaled * up_factor[...]).astype(BF16)
    for n, p in enumerate(order):
        outer(p, n == 0)

    sent(meta.at[0:nodes - 1], meta_send)
    sent(nraw.at[0:nodes - 1], raw_send.at[0])
    sent(zraw.at[0, 0:nodes - 1], raw_send.at[1])
    sent(zraw.at[0:locals_ - 1, 0], zraw_send)
    sent(zraw.at[0:locals_ - 1, 0:nodes - 1], plane_send)
    sent(cohort_meta.at[0:locals_ - 1], cmeta_send)
    for d in range(1, min(REACH, locals_ - 1) + 1):
        for s, there in enumerate((me_l + d < locals_, me_l >= d)):
            @pl.when(there)
            def _():
                sent(gath.at[0], pack_send.at[d - 1, s])
    for d in range(REACH, locals_ - 1):
        for s, (there, _, _) in enumerate(relays(d)):
            @pl.when(there)
            def _():
                sent(gath.at[0], relay_send.at[d - REACH, s])
    wtd_copy.wait_send()
    sent(peer_cot, cot_send)
    sent(share_buf.at[0:locals_ - 1], share_send)
    chosen = [one_hot(hits[j], before[j:j + 1], capacity) for j in range(exp_group)]
    received(back_buf.at[0:locals_ - 1], share_recv)
    route = []
    for j in range(exp_group):
        value = jnp.zeros((capacity, 1), F32)
        for o in range(owners):
            value = value + back_buf[j * owners + o, :, 0:1].astype(F32)
        route.append(jnp.sum(chosen[j] * value, axis=0, keepdims=True))
    route_out[...] = stacked(route)[0:exp_group].astype(BF16)


def write_kernel(gate_in, up_in, down_in, route_in, gate_to, up_to, down_to, route_to, sems):
    pairs = ((down_in, down_to), (gate_in, gate_to), (up_in, up_to), (route_in, route_to))
    copies = [pltpu.make_async_copy(src, dst, sems.at[t]) for t, (src, dst) in enumerate(pairs)]
    for copy in copies:
        copy.start()
    for copy in copies:
        copy.wait()


def gathered(nodes, locals_, group_tok, grad_out, expert_ids, route_weights, gate_pre, up_pre, w_down_t):
    tok, width = grad_out.shape
    top = expert_ids.shape[1]
    slots, hs = gate_pre.shape
    owners = H // hs
    exp_group = locals_ // owners
    cohort = nodes * tok
    capacity = slots // locals_
    half = width // 2
    pairs, near_width, far_width = column_pairs(half)
    near_pairs = sum(1 for pair in pairs if pair[0] == "near")
    far_pairs = len(pairs) - near_pairs
    dims = (nodes, locals_, tok, top, width, hs, group_tok, owners)
    dma = pltpu.SemaphoreType.DMA
    hbm = pl.BlockSpec(memory_space=pltpu.HBM)
    shapes = (
        jax.ShapeDtypeStruct((slots, hs), BF16),
        jax.ShapeDtypeStruct((slots, hs), BF16),
        jax.ShapeDtypeStruct((half, hs), BF16),
        jax.ShapeDtypeStruct((exp_group, cohort), BF16),
    )
    results = pl.pallas_call(
        functools.partial(routed_kernel, dims),
        out_shape=shapes,
        in_specs=[hbm] * 6,
        out_specs=tuple([pl.BlockSpec(memory_space=pltpu.VMEM)] * 4),
        scratch_shapes=[
            pltpu.VMEM((2 * slots, half), BF16),
            pltpu.VMEM((2 * slots, hs), BF16),
            pltpu.VMEM((top, tok), jnp.int32),
            pltpu.VMEM((top, tok), BF16),
            pltpu.VMEM((nodes, 2 * top, tok), F32),
            pltpu.VMEM((locals_, exp_group, cohort), F32),
            pltpu.VMEM((nodes, tok, near_width), BF16),
            pltpu.VMEM((locals_, group_tok, near_width), BF16),
            pltpu.VMEM((locals_, nodes, tok, far_width), BF16),
            pltpu.VMEM((slots, half), BF16),
            pltpu.VMEM((width, hs), BF16),
            pltpu.VMEM((2, slots, hs), BF16),
            pltpu.VMEM((slots, hs), F32),
            pltpu.VMEM((slots, hs), F32),
            pltpu.VMEM((slots, hs), F32),
            pltpu.VMEM((slots, hs), F32),
            pltpu.VMEM((locals_, capacity, 128), BF16),
            pltpu.VMEM((locals_, capacity, 128), BF16),
            dma((4,)), dma(()), dma((len(pairs),)),
            dma(()), dma(()), dma((2,)), dma((near_pairs,)),
            dma(()), dma((locals_, far_pairs)), dma(()), dma((far_pairs,)),
            dma((REACH, 2)), dma((locals_, near_pairs)), dma((max(1, locals_ - 1 - REACH), 2)),
            dma(()), dma(()),
            dma(()), dma(()), dma(()), dma((len(pairs),)), dma(()), dma(()),
        ],
        compiler_params=pltpu.CompilerParams(collective_id=0, has_side_effects=True, **KERNEL_PARAMS),
        name="routed",
    )(*[
        pltpu.with_memory_space_constraint(x, pltpu.HBM)
        for x in (expert_ids.T, route_weights.T, grad_out, gate_pre, up_pre, w_down_t)
    ])
    grad_gate, grad_up, grad_down, grad_route = pl.pallas_call(
        write_kernel,
        out_shape=shapes,
        in_specs=[pl.BlockSpec(memory_space=pl.ANY)] * 4,
        out_specs=tuple([pl.BlockSpec(memory_space=pl.ANY)] * 4),
        scratch_shapes=[dma((4,))],
        compiler_params=pltpu.CompilerParams(vmem_limit_bytes=1024 * 1024),
        name="write",
    )(*results)
    return grad_gate, grad_up, grad_down, grad_route.T


def swapped(block, axis, distance):
    count = lax.axis_size(axis)
    route = []
    for low in range(count):
        high = low | 1 << distance
        if high != low and high < count:
            route += [(low, high), (high, low)]
    return lax.ppermute(block, axis, route)


def outer_term(columns, weighted):
    return lax.dot_general(
        columns, weighted, (((0,), (0,)), ((), ())), preferred_element_type=jnp.float32
    )


def exchanged(grad_out, expert_ids, route_weights, gate_pre, up_pre, w_down_t):
    tok_dev, width = grad_out.shape
    slot_rows, hidden_slice = gate_pre.shape
    node_count = lax.axis_size("node")
    local_count = lax.axis_size("local")
    owners = H // hidden_slice
    exp_group = local_count // owners
    experts = exp_group * node_count
    capacity = slot_rows // local_count
    expert_range = lax.iota(jnp.int32, experts)
    route_hits = expert_ids[:, :, None] == expert_range[None, None, :]
    dense_weights = jnp.sum(
        jnp.where(route_hits, route_weights[:, :, None].astype(jnp.float32), 0.0), axis=1
    ).astype(jnp.bfloat16)
    cohort_grad, cohort_weights = (
        lax.all_gather(grad_out, "node", axis=0, tiled=True),
        lax.all_gather(dense_weights, "node", axis=0, tiled=True),
    )
    group_index = lax.axis_index("node")
    group_weights = lax.dynamic_slice_in_dim(cohort_weights, group_index * exp_group, exp_group, 1)
    routed = (group_weights != 0).astype(jnp.int32)
    position = lax.iota(jnp.int32, routed.shape[0])
    below = (position[:, None] > position[None, :]).astype(jnp.bfloat16)
    earlier = jnp.dot(below, routed.astype(jnp.bfloat16), preferred_element_type=jnp.float32).astype(jnp.int32)
    slot_range = lax.iota(jnp.int32, capacity)
    select = (routed[:, :, None] == 1) & (earlier[:, :, None] == slot_range[None, None, :])
    select_half = select.astype(jnp.bfloat16)
    packed = jnp.einsum(
        "cjs,cd->jsd", select_half, cohort_grad, preferred_element_type=jnp.float32
    ).astype(jnp.bfloat16)
    packed_weights = jnp.einsum(
        "cjs,cj->js", select_half, group_weights, preferred_element_type=jnp.float32
    ).astype(jnp.bfloat16)
    send_grad = jnp.broadcast_to(packed[:, None], (exp_group, owners, capacity, width)).reshape(
        local_count, capacity, width
    )
    send_weights = jnp.broadcast_to(packed_weights[:, None], (exp_group, owners, capacity)).reshape(
        local_count, capacity
    )
    recv_grad, recv_weights = (
        lax.all_to_all(send_grad, "local", split_axis=0, concat_axis=0, tiled=True),
        lax.all_to_all(send_weights, "local", split_axis=0, concat_axis=0, tiled=True),
    )
    cotangent = recv_grad.reshape(slot_rows, width)
    weight = recv_weights.reshape(slot_rows, 1).astype(jnp.float32)
    gate_value = gate_pre.astype(jnp.float32)
    up_value = up_pre.astype(jnp.float32)
    backward = jnp.dot(cotangent, w_down_t, preferred_element_type=jnp.float32)
    sigmoid_gate = jax.nn.sigmoid(gate_value)
    activated = gate_value * sigmoid_gate
    hidden = activated * up_value
    shares = jnp.sum(hidden * backward, axis=1).astype(jnp.bfloat16)
    scaled = weight * backward
    grad_gate_pre = (
        scaled * up_value * sigmoid_gate * (1.0 + gate_value * (1.0 - sigmoid_gate))
    ).astype(jnp.bfloat16)
    grad_up_pre = (scaled * activated).astype(jnp.bfloat16)
    weighted = (weight * hidden).astype(jnp.bfloat16)
    returned = lax.all_to_all(
        shares.reshape(local_count, capacity), "local", split_axis=0, concat_axis=0, tiled=True
    )
    slice_sum = jnp.sum(returned.astype(jnp.float32).reshape(exp_group, owners, capacity), axis=1)
    grad_route = jnp.sum(jnp.where(select, slice_sum[None], 0.0), axis=2).astype(jnp.bfloat16)
    half_width = width // lax.axis_size("rep")
    replica = lax.axis_index("rep")
    own_cols = lax.dynamic_slice_in_dim(cotangent, replica * half_width, half_width, 1)
    peer_cols = lax.dynamic_slice_in_dim(cotangent, (1 - replica) * half_width, half_width, 1)
    got_cols, got_weighted = swapped((peer_cols, weighted), "rep", 0)
    own_term = outer_term(own_cols, weighted).astype(jnp.bfloat16).astype(jnp.float32)
    peer_term = outer_term(got_cols, got_weighted).astype(jnp.bfloat16).astype(jnp.float32)
    grad_down_t = (own_term + peer_term).astype(jnp.bfloat16)
    return (grad_gate_pre, grad_up_pre, grad_down_t, grad_route)


def per_device(grad_out, expert_ids, route_weights, gate_pre, up_pre, w_down_t):
    nodes, locals_ = lax.axis_size("node"), lax.axis_size("local")
    capacity = gate_pre.shape[0] // locals_
    group_tok = grad_out.shape[0] * expert_ids.shape[1] // PER_GROUP
    args = (grad_out, expert_ids, route_weights, gate_pre, up_pre, w_down_t)
    if group_tok > capacity:
        return exchanged(*args)
    return gathered(nodes, locals_, group_tok, *args)


def solution(mesh):
    placed = (
        P(("node", "local", "rep"), None),
        P(("node", "local", "rep"), None),
        P(("node", "local", "rep"), None),
        P("rep", ("node", "local")),
        P("rep", ("node", "local")),
        P(None, ("node", "local")),
    )
    return jax.shard_map(
        per_device,
        mesh=mesh,
        in_specs=placed,
        out_specs=(
            P("rep", ("node", "local")),
            P("rep", ("node", "local")),
            P("rep", ("node", "local")),
            P(("local", "rep"), "node"),
        ),
        check_vma=False,
    )
```

```python
import functools
import jax
import jax.numpy as jnp
from jax import lax
from jax.experimental import pallas as pl
from jax.experimental.pallas import tpu as pltpu
from jax.sharding import PartitionSpec as P

H = 1024
PER_GROUP = 2
PAIRS = (("near", 4), ("far", 4), ("near", 4), ("far", 4))
TILE = 256
REACH = 2
MESH = pl.DeviceIdType.MESH
F32 = jnp.float32
BF16 = jnp.bfloat16
KERNEL_PARAMS = dict(vmem_limit_bytes=40 * 1024 * 1024)


def contract_rows(left, right):
    return lax.dot_general(left, right, (((0,), (0,)), ((), ())), preferred_element_type=F32)


def one_hot(member, row, height):
    places = lax.broadcasted_iota(jnp.int32, (height, member.shape[1]), 0).astype(F32)
    return jnp.where((member > 0) & (row == places), 1.0, 0.0)


def earlier_counts(rows, block):
    count = rows.shape[1]
    above = lax.broadcasted_iota(jnp.int32, (count, count), 0)
    col = lax.broadcasted_iota(jnp.int32, (count, count), 1)
    strict = jnp.where((above < col) & (above // block == col // block), 1.0, 0.0).astype(BF16)
    return jnp.dot(rows.astype(BF16), strict, preferred_element_type=F32)


def stacked(rows):
    lines = lax.broadcasted_iota(jnp.int32, (8, rows[0].shape[1]), 0)
    out = jnp.zeros(lines.shape, F32)
    for place, row in enumerate(rows):
        out = jnp.where(lines == place, row, out)
    return out


def column_pairs(half):
    parts = sum(share for _, share in PAIRS)
    pairs, taken, at = [], {"near": 0, "far": 0}, 0
    for way, share in PAIRS:
        size = half * share // parts
        pairs.append((way, at, size, taken[way]))
        taken[way] += 2 * size
        at += size
    return pairs, taken["near"], taken["far"]


def routed_kernel(
    dims, ids_ref, rw_ref, grad_ref, gate_ref, up_ref, w_ref,
    ggate_out, gup_out, down_out, route_out,
    near_mix, far_mix, ids_buf, rw_buf, meta, cohort_meta, nraw, gath, zraw, far_rows, near_peer, far_peer, w_buf, gate_up,
    near_acc, far_acc, hidden_buf, gate_factor, up_factor, share_buf, back_buf,
    own_sem, load_sem, w_sem,
    meta_send, meta_recv, raw_send, nraw_recv, zraw_send, zraw_recv, plane_send, plane_recv,
    pack_send, pack_recv, relay_send, cmeta_send, cmeta_recv,
    mix_send, mix_recv, rows_send, rows_recv, share_send, share_recv, turn,
):
    nodes, locals_, tok, top, width, hs, group_tok, owners = dims
    cohort = nodes * tok
    exp_group = locals_ // owners
    slots = gate_ref.shape[0]
    capacity = slots // locals_
    half = width // 2
    pairs, near_width, far_width = column_pairs(half)
    near = [p for p, pair in enumerate(pairs) if pair[0] == "near"]
    far = [p for p, pair in enumerate(pairs) if pair[0] == "far"]
    me_n, me_l, me_r = lax.axis_index("node"), lax.axis_index("local"), lax.axis_index("rep")
    peer = {"rep": 1 - me_r}

    def node_at(k):
        return {"node": lax.rem(me_n + k, nodes)}

    def local_at(k):
        return {"local": lax.rem(me_l + k, locals_)}

    def remote(src, dst, send, recv, device):
        return pltpu.make_async_remote_copy(
            src_ref=src, dst_ref=dst, send_sem=send, recv_sem=recv,
            device_id=device, device_id_type=MESH,
        )

    def received(ref, sem):
        remote(ref, ref, sem, sem, peer).wait_recv()

    def sent(ref, sem):
        remote(ref, ref, sem, sem, peer).wait_send()

    barrier = pltpu.get_barrier_semaphore()
    for k in range(1, nodes):
        pl.semaphore_signal(barrier, inc=1, device_id=node_at(k), device_id_type=MESH)
    for k in range(1, locals_):
        pl.semaphore_signal(barrier, inc=1, device_id=local_at(k), device_id_type=MESH)
    pl.semaphore_signal(barrier, inc=1, device_id=peer, device_id_type=MESH)

    def block(p):
        return pl.ds(pairs[p][3], 2 * pairs[p][2])

    def part(p):
        return pl.ds(pairs[p][1], pairs[p][2])

    id_copy = pltpu.make_async_copy(ids_ref, ids_buf, own_sem.at[0])
    rw_copy = pltpu.make_async_copy(rw_ref, rw_buf, own_sem.at[1])
    id_copy.start()
    rw_copy.start()
    for p, (way, at, size, place) in enumerate(pairs):
        for h in range(2):
            here = pl.ds(place + h * size, size)
            target = nraw.at[me_n, :, here] if way == "near" else zraw.at[me_l, me_n, :, here]
            pltpu.make_async_copy(
                grad_ref.at[:, pl.ds(h * half + at, size)], target, own_sem.at[2 if way == "near" else 3]
            ).start()
    pltpu.make_async_copy(gate_ref, gate_up.at[0], load_sem).start()
    pltpu.make_async_copy(up_ref, gate_up.at[1], load_sem).start()
    id_copy.wait()
    rw_copy.wait()
    meta[me_n, 0:top, :] = ids_buf[...].astype(F32)
    meta[me_n, top:2 * top, :] = rw_buf[...].astype(F32)
    own_near, own_far = nraw.at[me_n], zraw.at[me_l, me_n]
    pltpu.make_async_copy(own_near, own_near, own_sem.at[2]).wait()
    pltpu.make_async_copy(own_far, own_far, own_sem.at[3]).wait()
    pl.semaphore_wait(barrier, nodes + locals_ - 1)

    for k in range(1, nodes):
        remote(meta.at[me_n], meta.at[me_n], meta_send, meta_recv, node_at(k)).start()

    def beside(d):
        return [(me_l >= d, me_l - d), (me_l + d < locals_, me_l + d)]

    def far_block(l, n, p):
        return zraw.at[l, n, :, block(p)]

    for i, p in enumerate(near):
        for k in range(1, nodes):
            own = nraw.at[me_n, :, block(p)]
            remote(own, own, raw_send.at[0], nraw_recv.at[i], node_at(k)).start()
    @pl.when(me_r == 1)
    def _():
        pl.semaphore_wait(turn, 1)

    for i, p in enumerate(far):
        for d in range(1, locals_):
            for there, target in beside(d):
                @pl.when(there)
                def _():
                    own = far_block(me_l, me_n, p)
                    remote(own, own, zraw_send, zraw_recv.at[me_l, i], {"local": target}).start()
    for i, p in enumerate(far):
        for k in range(1, nodes):
            own = far_block(me_l, me_n, p)
            remote(own, own, raw_send.at[1], plane_recv.at[i], node_at(k)).start()

    @pl.when(me_r == 0)
    def _():
        pl.semaphore_signal(turn, inc=1, device_id=peer, device_id_type=MESH)

    w_at = 0
    w_rows = []
    for p, (way, at, size, place) in enumerate(pairs):
        for h in range(2):
            pltpu.make_async_copy(
                w_ref.at[pl.ds(h * half + at, size), :], w_buf.at[pl.ds(w_at + h * size, size), :], w_sem.at[p]
            ).start()
        w_rows.append(pl.ds(w_at, 2 * size))
        w_at += 2 * size

    pltpu.make_async_copy(gate_up, gate_up, load_sem).wait()
    gate, up = gate_up[0].astype(F32), gate_up[1].astype(F32)
    sig = jax.nn.sigmoid(gate)
    act = gate * sig
    hidden_buf[...] = act * up
    up_factor[...] = act
    gate_factor[...] = up * sig * (1.0 + gate * (1.0 - sig))

    received(meta.at[0:nodes - 1], meta_recv)
    own_meta = jnp.concatenate([meta[n] for n in range(nodes)], axis=1)
    own_ids, own_rw = own_meta[0:top], own_meta[top:2 * top]
    low = (me_n * exp_group).astype(F32)
    named = [jnp.where(own_ids == low + j, 1.0, 0.0) for j in range(exp_group)]
    hits = [jnp.sum(match, axis=0, keepdims=True) for match in named]
    in_group = jnp.where(sum(hits) > 0, 1.0, 0.0)
    before = earlier_counts(stacked(hits + [in_group]), cohort)
    pick = one_hot(in_group, before[exp_group:exp_group + 1], group_tok).astype(BF16)

    def send_pack(i):
        p = near[i]
        received(nraw.at[0:nodes - 1, :, block(p)], nraw_recv.at[i])
        rows = nraw[:, :, block(p)].reshape(cohort, 2 * pairs[p][2])
        gath[me_l, :, block(p)] = jnp.dot(pick, rows, preferred_element_type=F32).astype(BF16)
        own = gath.at[me_l, :, block(p)]
        for d in range(locals_ - 1, 0, -1):
            for s, (there, target) in enumerate([(me_l + d < locals_, me_l + d), (me_l >= d, me_l - d)]):
                if d > REACH:
                    there = there & (me_r == 0)

                @pl.when(there)
                def _():
                    remote(own, own, pack_send.at[d - 1, s], pack_recv.at[me_l, i], {"local": target}).start()

    def send_cohort_meta():
        weights = [jnp.sum(match * own_rw, axis=0, keepdims=True) for match in named]
        cohort_meta[me_l] = stacked(weights)[0:exp_group]
        for k in range(1, locals_):
            own = cohort_meta.at[me_l]
            remote(own, own, cmeta_send, cmeta_recv, local_at(k)).start()

    def relays(d):
        return [
            ((me_r == 1) & (me_l >= d) & (me_l + 1 < locals_), me_l - d, me_l + 1),
            ((me_r == 1) & (me_l + d < locals_) & (me_l >= 1), me_l + d, me_l - 1),
        ]

    def relay_pack(i, d):
        for s, (there, source, target) in enumerate(relays(d)):
            @pl.when(there)
            def _():
                pack = gath.at[source, :, block(near[i])]
                received(pack, pack_recv.at[source, i])
                remote(pack, pack, relay_send.at[d - REACH, s], pack_recv.at[source, i], {"local": target}).start()

    def forward(i, d):
        p = far[i]
        for there, source in beside(d):
            @pl.when(there)
            def _():
                piece = far_block(source, me_n, p)
                received(piece, zraw_recv.at[source, i])
                for k in range(1, nodes):
                    remote(piece, piece, plane_send, plane_recv.at[i], node_at(k)).start()

    state = {}

    def prepare():
        received(cohort_meta.at[0:locals_ - 1], cmeta_recv)
        total = locals_ * cohort
        weights = jnp.concatenate([cohort_meta[l] for l in range(locals_)], axis=1)
        mine = lax.broadcasted_iota(jnp.int32, (exp_group, total), 0) == me_l // owners
        row_weight = jnp.sum(jnp.where(mine, weights, 0.0), axis=0, keepdims=True)
        member = jnp.where(row_weight > 0, 1.0, 0.0)
        grouped = jnp.where(jnp.sum(weights, axis=0, keepdims=True) > 0, 1.0, 0.0)
        earlier = earlier_counts(stacked([member, grouped]), cohort)
        which = (lax.broadcasted_iota(jnp.int32, (1, total), 1) // cohort).astype(F32)
        slot_hot = one_hot(member, earlier[0:1] + which * capacity, slots)
        pack_hot = one_hot(grouped, earlier[1:2] + which * group_tok, locals_ * group_tok)
        state["far"] = slot_hot.astype(BF16)
        state["near"] = lax.dot_general(
            slot_hot.astype(BF16), pack_hot.astype(BF16),
            (((1,), (1,)), ((), ())), preferred_element_type=F32,
        ).astype(BF16)
        weight = jnp.sum(slot_hot * row_weight, axis=1, keepdims=True)
        state["weight"] = weight
        weighted = (weight * hidden_buf[...]).astype(BF16)
        for way, mix in mixes.items():
            rows = mix.shape[0] // 2
            mix[0:rows, :] = contract_rows(state[way], weighted).astype(BF16)
            mix_copy(way).start()

    mixes = {"near": near_mix, "far": far_mix}
    ways = ("near", "far")

    def mix_copy(way):
        mix, w = mixes[way], ways.index(way)
        rows = mix.shape[0] // 2
        return remote(mix.at[0:rows, :], mix.at[rows:2 * rows, :], mix_send.at[w], mix_recv.at[w], peer)

    def half_of(p, r):
        return pl.ds(pl.multiple_of(pairs[p][3] + r * pairs[p][2], 128), pairs[p][2])

    def peer_part(p):
        return pl.ds(pairs[p][3] // 2, pairs[p][2])

    def rows_copy(p):
        w, there = ways.index(pairs[p][0]), half_of(p, 1 - me_r)
        if w == 0:
            return remote(gath.at[:, :, there], near_peer.at[:, :, peer_part(p)], rows_send.at[w], rows_recv.at[p], peer)
        return remote(far_rows.at[:, there], far_peer.at[:, peer_part(p)], rows_send.at[w], rows_recv.at[p], peer)

    def arrived(p):
        if pairs[p][0] == "far":
            received(zraw.at[:, 0:nodes - 1, :, block(p)], plane_recv.at[far.index(p)])
            return
        i = near.index(p)
        for d in range(1, locals_):
            for s, (there, source) in enumerate(beside(d)):
                if REACH <= d < locals_ - 1:
                    there = there & jnp.logical_not(relays(d)[s][0])

                @pl.when(there)
                def _():
                    received(gath.at[source, :, block(p)], pack_recv.at[source, i])

    def finish(p):
        way, at, size, place = pairs[p]
        arrived(p)
        if way == "far":
            rows = zraw[:, :, :, block(p)].reshape(locals_ * cohort, 2 * size)
            far_rows[:, block(p)] = rows
        else:
            rows = gath[:, :, block(p)].reshape(locals_ * group_tok, 2 * size)
        rows_copy(p).start()
        w_part = w_buf.at[w_rows[p], :]
        pltpu.make_async_copy(w_part, w_part, w_sem.at[p]).wait()
        term = jnp.dot(rows, w_buf[w_rows[p], :], preferred_element_type=F32)
        total = near_acc if way == "near" else far_acc
        if p == (near if way == "near" else far)[0]:
            total[...] = term
        else:
            total[...] += term

    def selected(way, total):
        high = total.astype(BF16)
        low_part = (total - high.astype(F32)).astype(BF16)
        return (
            jnp.dot(state[way], high, preferred_element_type=F32)
            + jnp.dot(state[way], low_part, preferred_element_type=F32)
        )

    def outer(p, fresh):
        way, at, size, place = pairs[p]
        if fresh:
            mix_copy(way).wait_recv()
        rows_copy(p).wait_recv()
        for t in range(0, size, TILE):
            wide = min(TILE, size - t)
            mine = pl.ds(pl.multiple_of(place + me_r * size + t, 128), wide)
            theirs = pl.ds(place // 2 + t, wide)
            if way == "near":
                pieces = [
                    gath[:, :, mine].reshape(locals_ * group_tok, wide),
                    near_peer[:, :, theirs].reshape(locals_ * group_tok, wide),
                ]
            else:
                pieces = [far_rows[:, mine], far_peer[:, theirs]]
            down_out[pl.ds(at + t, wide), :] = contract_rows(
                jnp.concatenate(pieces, axis=0), mixes[way][...]
            ).astype(BF16)

    send_cohort_meta()
    send_pack(0)
    forward(0, 1)
    send_pack(1)
    forward(1, 1)
    forward(0, 2)
    forward(1, 2)
    forward(0, 3)
    forward(1, 3)
    relay_pack(0, 2)
    relay_pack(1, 2)
    prepare()
    order = [near[0], far[0], near[1], far[1]]
    for n, p in enumerate(order):
        finish(p)
        if p == near[-1]:
            near_back = selected("near", near_acc[...])

    back = near_back + selected("far", far_acc[...])
    shares = jnp.sum(hidden_buf[...] * back, axis=1, keepdims=True)
    share_buf[...] = jnp.broadcast_to(shares, (slots, 128)).astype(BF16).reshape(locals_, capacity, 128)
    for k in range(1, locals_):
        remote(
            share_buf.at[lax.rem(me_l + k, locals_)], back_buf.at[me_l], share_send, share_recv, local_at(k)
        ).start()
    back_buf[me_l] = share_buf[me_l]
    scaled = state["weight"] * back
    ggate_out[...] = (scaled * gate_factor[...]).astype(BF16)
    gup_out[...] = (scaled * up_factor[...]).astype(BF16)
    for p in order:
        outer(p, p in (near[0], far[0]))

    sent(meta.at[0:nodes - 1], meta_send)
    sent(nraw.at[0:nodes - 1], raw_send.at[0])
    sent(zraw.at[0, 0:nodes - 1], raw_send.at[1])
    sent(zraw.at[0:locals_ - 1, 0], zraw_send)
    sent(zraw.at[0:locals_ - 1, 0:nodes - 1], plane_send)
    sent(cohort_meta.at[0:locals_ - 1], cmeta_send)
    for d in range(1, locals_):
        for s, there in enumerate((me_l + d < locals_, me_l >= d)):
            if d > REACH:
                there = there & (me_r == 0)

            @pl.when(there)
            def _():
                sent(gath.at[0], pack_send.at[d - 1, s])
    for d in range(REACH, locals_ - 1):
        for s, (there, _, _) in enumerate(relays(d)):
            @pl.when(there)
            def _():
                sent(gath.at[0], relay_send.at[d - REACH, s])
    for way in ways:
        mix_copy(way).wait_send()
    sent(near_peer, rows_send.at[0])
    sent(far_peer, rows_send.at[1])
    sent(share_buf.at[0:locals_ - 1], share_send)
    chosen = [one_hot(hits[j], before[j:j + 1], capacity) for j in range(exp_group)]
    received(back_buf.at[0:locals_ - 1], share_recv)
    route = []
    for j in range(exp_group):
        value = jnp.zeros((capacity, 1), F32)
        for o in range(owners):
            value = value + back_buf[j * owners + o, :, 0:1].astype(F32)
        route.append(jnp.sum(chosen[j] * value, axis=0, keepdims=True))
    route_out[...] = stacked(route)[0:exp_group].astype(BF16)


def write_kernel(gate_in, up_in, down_in, route_in, gate_to, up_to, down_to, route_to, sems):
    pairs = ((down_in, down_to), (gate_in, gate_to), (up_in, up_to), (route_in, route_to))
    copies = [pltpu.make_async_copy(src, dst, sems.at[t]) for t, (src, dst) in enumerate(pairs)]
    for copy in copies:
        copy.start()
    for copy in copies:
        copy.wait()


def gathered(nodes, locals_, group_tok, grad_out, expert_ids, route_weights, gate_pre, up_pre, w_down_t):
    tok, width = grad_out.shape
    top = expert_ids.shape[1]
    slots, hs = gate_pre.shape
    owners = H // hs
    exp_group = locals_ // owners
    cohort = nodes * tok
    capacity = slots // locals_
    half = width // 2
    pairs, near_width, far_width = column_pairs(half)
    near_pairs = sum(1 for pair in pairs if pair[0] == "near")
    far_pairs = len(pairs) - near_pairs
    dims = (nodes, locals_, tok, top, width, hs, group_tok, owners)
    dma = pltpu.SemaphoreType.DMA
    hbm = pl.BlockSpec(memory_space=pltpu.HBM)
    shapes = (
        jax.ShapeDtypeStruct((slots, hs), BF16),
        jax.ShapeDtypeStruct((slots, hs), BF16),
        jax.ShapeDtypeStruct((half, hs), BF16),
        jax.ShapeDtypeStruct((exp_group, cohort), BF16),
    )
    results = pl.pallas_call(
        functools.partial(routed_kernel, dims),
        out_shape=shapes,
        in_specs=[hbm] * 6,
        out_specs=tuple([pl.BlockSpec(memory_space=pltpu.VMEM)] * 4),
        scratch_shapes=[
            pltpu.VMEM((2 * locals_ * group_tok, hs), BF16),
            pltpu.VMEM((2 * locals_ * cohort, hs), BF16),
            pltpu.VMEM((top, tok), jnp.int32),
            pltpu.VMEM((top, tok), BF16),
            pltpu.VMEM((nodes, 2 * top, tok), F32),
            pltpu.VMEM((locals_, exp_group, cohort), F32),
            pltpu.VMEM((nodes, tok, near_width), BF16),
            pltpu.VMEM((locals_, group_tok, near_width), BF16),
            pltpu.VMEM((locals_, nodes, tok, far_width), BF16),
            pltpu.VMEM((locals_ * cohort, far_width), BF16),
            pltpu.VMEM((locals_, group_tok, near_width // 2), BF16),
            pltpu.VMEM((locals_ * cohort, far_width // 2), BF16),
            pltpu.VMEM((width, hs), BF16),
            pltpu.VMEM((2, slots, hs), BF16),
            pltpu.VMEM((locals_ * group_tok, hs), F32),
            pltpu.VMEM((locals_ * cohort, hs), F32),
            pltpu.VMEM((slots, hs), F32),
            pltpu.VMEM((slots, hs), F32),
            pltpu.VMEM((slots, hs), F32),
            pltpu.VMEM((locals_, capacity, 128), BF16),
            pltpu.VMEM((locals_, capacity, 128), BF16),
            dma((4,)), dma(()), dma((len(pairs),)),
            dma(()), dma(()), dma((2,)), dma((near_pairs,)),
            dma(()), dma((locals_, far_pairs)), dma(()), dma((far_pairs,)),
            dma((locals_ - 1, 2)), dma((locals_, near_pairs)), dma((max(1, locals_ - 1 - REACH), 2)),
            dma(()), dma(()),
            dma((2,)), dma((2,)), dma((2,)), dma((len(pairs),)), dma(()), dma(()), pltpu.SemaphoreType.REGULAR,
        ],
        compiler_params=pltpu.CompilerParams(collective_id=0, has_side_effects=True, **KERNEL_PARAMS),
        name="routed",
    )(*[
        pltpu.with_memory_space_constraint(x, pltpu.HBM)
        for x in (expert_ids.T, route_weights.T, grad_out, gate_pre, up_pre, w_down_t)
    ])
    grad_gate, grad_up, grad_down, grad_route = pl.pallas_call(
        write_kernel,
        out_shape=shapes,
        in_specs=[pl.BlockSpec(memory_space=pl.ANY)] * 4,
        out_specs=tuple([pl.BlockSpec(memory_space=pl.ANY)] * 4),
        scratch_shapes=[dma((4,))],
        compiler_params=pltpu.CompilerParams(vmem_limit_bytes=1024 * 1024),
        name="write",
    )(*results)
    return grad_gate, grad_up, grad_down, grad_route.T


def swapped(block, axis, distance):
    count = lax.axis_size(axis)
    route = []
    for low in range(count):
        high = low | 1 << distance
        if high != low and high < count:
            route += [(low, high), (high, low)]
    return lax.ppermute(block, axis, route)


def outer_term(columns, weighted):
    return lax.dot_general(
        columns, weighted, (((0,), (0,)), ((), ())), preferred_element_type=jnp.float32
    )


def exchanged(grad_out, expert_ids, route_weights, gate_pre, up_pre, w_down_t):
    tok_dev, width = grad_out.shape
    slot_rows, hidden_slice = gate_pre.shape
    node_count = lax.axis_size("node")
    local_count = lax.axis_size("local")
    owners = H // hidden_slice
    exp_group = local_count // owners
    experts = exp_group * node_count
    capacity = slot_rows // local_count
    expert_range = lax.iota(jnp.int32, experts)
    route_hits = expert_ids[:, :, None] == expert_range[None, None, :]
    dense_weights = jnp.sum(
        jnp.where(route_hits, route_weights[:, :, None].astype(jnp.float32), 0.0), axis=1
    ).astype(jnp.bfloat16)
    cohort_grad, cohort_weights = (
        lax.all_gather(grad_out, "node", axis=0, tiled=True),
        lax.all_gather(dense_weights, "node", axis=0, tiled=True),
    )
    group_index = lax.axis_index("node")
    group_weights = lax.dynamic_slice_in_dim(cohort_weights, group_index * exp_group, exp_group, 1)
    routed = (group_weights != 0).astype(jnp.int32)
    position = lax.iota(jnp.int32, routed.shape[0])
    below = (position[:, None] > position[None, :]).astype(jnp.bfloat16)
    earlier = jnp.dot(below, routed.astype(jnp.bfloat16), preferred_element_type=jnp.float32).astype(jnp.int32)
    slot_range = lax.iota(jnp.int32, capacity)
    select = (routed[:, :, None] == 1) & (earlier[:, :, None] == slot_range[None, None, :])
    select_half = select.astype(jnp.bfloat16)
    packed = jnp.einsum(
        "cjs,cd->jsd", select_half, cohort_grad, preferred_element_type=jnp.float32
    ).astype(jnp.bfloat16)
    packed_weights = jnp.einsum(
        "cjs,cj->js", select_half, group_weights, preferred_element_type=jnp.float32
    ).astype(jnp.bfloat16)
    send_grad = jnp.broadcast_to(packed[:, None], (exp_group, owners, capacity, width)).reshape(
        local_count, capacity, width
    )
    send_weights = jnp.broadcast_to(packed_weights[:, None], (exp_group, owners, capacity)).reshape(
        local_count, capacity
    )
    recv_grad, recv_weights = (
        lax.all_to_all(send_grad, "local", split_axis=0, concat_axis=0, tiled=True),
        lax.all_to_all(send_weights, "local", split_axis=0, concat_axis=0, tiled=True),
    )
    cotangent = recv_grad.reshape(slot_rows, width)
    weight = recv_weights.reshape(slot_rows, 1).astype(jnp.float32)
    gate_value = gate_pre.astype(jnp.float32)
    up_value = up_pre.astype(jnp.float32)
    backward = jnp.dot(cotangent, w_down_t, preferred_element_type=jnp.float32)
    sigmoid_gate = jax.nn.sigmoid(gate_value)
    activated = gate_value * sigmoid_gate
    hidden = activated * up_value
    shares = jnp.sum(hidden * backward, axis=1).astype(jnp.bfloat16)
    scaled = weight * backward
    grad_gate_pre = (
        scaled * up_value * sigmoid_gate * (1.0 + gate_value * (1.0 - sigmoid_gate))
    ).astype(jnp.bfloat16)
    grad_up_pre = (scaled * activated).astype(jnp.bfloat16)
    weighted = (weight * hidden).astype(jnp.bfloat16)
    returned = lax.all_to_all(
        shares.reshape(local_count, capacity), "local", split_axis=0, concat_axis=0, tiled=True
    )
    slice_sum = jnp.sum(returned.astype(jnp.float32).reshape(exp_group, owners, capacity), axis=1)
    grad_route = jnp.sum(jnp.where(select, slice_sum[None], 0.0), axis=2).astype(jnp.bfloat16)
    half_width = width // lax.axis_size("rep")
    replica = lax.axis_index("rep")
    own_cols = lax.dynamic_slice_in_dim(cotangent, replica * half_width, half_width, 1)
    peer_cols = lax.dynamic_slice_in_dim(cotangent, (1 - replica) * half_width, half_width, 1)
    got_cols, got_weighted = swapped((peer_cols, weighted), "rep", 0)
    own_term = outer_term(own_cols, weighted).astype(jnp.bfloat16).astype(jnp.float32)
    peer_term = outer_term(got_cols, got_weighted).astype(jnp.bfloat16).astype(jnp.float32)
    grad_down_t = (own_term + peer_term).astype(jnp.bfloat16)
    return (grad_gate_pre, grad_up_pre, grad_down_t, grad_route)


def per_device(grad_out, expert_ids, route_weights, gate_pre, up_pre, w_down_t):
    nodes, locals_ = lax.axis_size("node"), lax.axis_size("local")
    capacity = gate_pre.shape[0] // locals_
    group_tok = grad_out.shape[0] * expert_ids.shape[1] // PER_GROUP
    args = (grad_out, expert_ids, route_weights, gate_pre, up_pre, w_down_t)
    if group_tok > capacity:
        return exchanged(*args)
    return gathered(nodes, locals_, group_tok, *args)


def solution(mesh):
    placed = (
        P(("node", "local", "rep"), None),
        P(("node", "local", "rep"), None),
        P(("node", "local", "rep"), None),
        P("rep", ("node", "local")),
        P("rep", ("node", "local")),
        P(None, ("node", "local")),
    )
    return jax.shard_map(
        per_device,
        mesh=mesh,
        in_specs=placed,
        out_specs=(
            P("rep", ("node", "local")),
            P("rep", ("node", "local")),
            P("rep", ("node", "local")),
            P(("local", "rep"), "node"),
        ),
        check_vma=False,
    )
```

```python
import functools
import jax
import jax.numpy as jnp
from jax import lax
from jax.experimental import pallas as pl
from jax.experimental.pallas import tpu as pltpu
from jax.sharding import PartitionSpec as P

H = 1024
PER_GROUP = 2
PAIRS = (("near", 4), ("far", 4), ("near", 4), ("far", 4))
TILE = 256
REACH = 2
MESH = pl.DeviceIdType.MESH
F32 = jnp.float32
BF16 = jnp.bfloat16
KERNEL_PARAMS = dict(vmem_limit_bytes=40 * 1024 * 1024)


def contract_rows(left, right):
    return lax.dot_general(left, right, (((0,), (0,)), ((), ())), preferred_element_type=F32)


def one_hot(member, row, height):
    places = lax.broadcasted_iota(jnp.int32, (height, member.shape[1]), 0).astype(F32)
    return jnp.where((member > 0) & (row == places), 1.0, 0.0)


def earlier_counts(rows, block):
    count = rows.shape[1]
    above = lax.broadcasted_iota(jnp.int32, (count, count), 0)
    col = lax.broadcasted_iota(jnp.int32, (count, count), 1)
    strict = jnp.where((above < col) & (above // block == col // block), 1.0, 0.0).astype(BF16)
    return jnp.dot(rows.astype(BF16), strict, preferred_element_type=F32)


def stacked(rows):
    lines = lax.broadcasted_iota(jnp.int32, (8, rows[0].shape[1]), 0)
    out = jnp.zeros(lines.shape, F32)
    for place, row in enumerate(rows):
        out = jnp.where(lines == place, row, out)
    return out


def column_pairs(half):
    parts = sum(share for _, share in PAIRS)
    pairs, taken, at = [], {"near": 0, "far": 0}, 0
    for way, share in PAIRS:
        size = half * share // parts
        pairs.append((way, at, size, taken[way]))
        taken[way] += 2 * size
        at += size
    return pairs, taken["near"], taken["far"]


def routed_kernel(
    dims, ids_ref, rw_ref, grad_ref, gate_ref, up_ref, w_ref,
    ggate_out, gup_out, down_out, route_out,
    mix, ids_buf, rw_buf, meta, cohort_meta, nraw, gath, zraw, far_rows, near_peer, far_peer, w_buf, gate_up,
    acc, hidden_buf, gate_factor, up_factor, share_buf, back_buf,
    own_sem, load_sem, w_sem,
    meta_send, meta_recv, raw_send, nraw_recv, zraw_send, zraw_recv, plane_send, plane_recv,
    pack_send, pack_recv, relay_recv, cmeta_send, cmeta_recv,
    mix_send, mix_recv, rows_send, rows_recv, share_send, share_recv, turn,
):
    nodes, locals_, tok, top, width, hs, group_tok, owners = dims
    cohort = nodes * tok
    exp_group = locals_ // owners
    slots = gate_ref.shape[0]
    capacity = slots // locals_
    half = width // 2
    pairs, near_width, far_width = column_pairs(half)
    near = [p for p, pair in enumerate(pairs) if pair[0] == "near"]
    far = [p for p, pair in enumerate(pairs) if pair[0] == "far"]
    me_n, me_l, me_r = lax.axis_index("node"), lax.axis_index("local"), lax.axis_index("rep")
    peer = {"rep": 1 - me_r}

    def node_at(k):
        return {"node": lax.rem(me_n + k, nodes)}

    def local_at(k):
        return {"local": lax.rem(me_l + k, locals_)}

    def remote(src, dst, send, recv, device):
        return pltpu.make_async_remote_copy(
            src_ref=src, dst_ref=dst, send_sem=send, recv_sem=recv,
            device_id=device, device_id_type=MESH,
        )

    def received(ref, sem):
        remote(ref, ref, sem, sem, peer).wait_recv()

    def sent(ref, sem):
        remote(ref, ref, sem, sem, peer).wait_send()

    barrier = pltpu.get_barrier_semaphore()
    for k in range(1, nodes):
        pl.semaphore_signal(barrier, inc=1, device_id=node_at(k), device_id_type=MESH)
    for k in range(1, locals_):
        pl.semaphore_signal(barrier, inc=1, device_id=local_at(k), device_id_type=MESH)
    pl.semaphore_signal(barrier, inc=1, device_id=peer, device_id_type=MESH)

    def block(p):
        return pl.ds(pairs[p][3], 2 * pairs[p][2])

    def part(p):
        return pl.ds(pairs[p][1], pairs[p][2])

    id_copy = pltpu.make_async_copy(ids_ref, ids_buf, own_sem.at[0])
    rw_copy = pltpu.make_async_copy(rw_ref, rw_buf, own_sem.at[1])
    id_copy.start()
    rw_copy.start()
    for p, (way, at, size, place) in enumerate(pairs):
        for h in range(2):
            here = pl.ds(place + h * size, size)
            target = nraw.at[me_n, :, here] if way == "near" else zraw.at[me_l, me_n, :, here]
            pltpu.make_async_copy(
                grad_ref.at[:, pl.ds(h * half + at, size)], target, own_sem.at[2 if way == "near" else 3]
            ).start()
    pltpu.make_async_copy(gate_ref, gate_up.at[0], load_sem).start()
    pltpu.make_async_copy(up_ref, gate_up.at[1], load_sem).start()
    id_copy.wait()
    rw_copy.wait()
    meta[me_n, 0:top, :] = ids_buf[...].astype(F32)
    meta[me_n, top:2 * top, :] = rw_buf[...].astype(F32)
    own_near, own_far = nraw.at[me_n], zraw.at[me_l, me_n]
    pltpu.make_async_copy(own_near, own_near, own_sem.at[2]).wait()
    pltpu.make_async_copy(own_far, own_far, own_sem.at[3]).wait()
    pl.semaphore_wait(barrier, nodes + locals_ - 1)

    for k in range(1, nodes):
        remote(meta.at[me_n], meta.at[me_n], meta_send, meta_recv, node_at(k)).start()

    def beside(d):
        return [(me_l >= d, me_l - d), (me_l + d < locals_, me_l + d)]

    def far_block(l, n, p):
        return zraw.at[l, n, :, block(p)]

    for i, p in enumerate(near):
        for k in range(1, nodes):
            own = nraw.at[me_n, :, block(p)]
            remote(own, own, raw_send, nraw_recv.at[i], node_at(k)).start()
    @pl.when(me_r == 1)
    def _():
        pl.semaphore_wait(turn, 1)

    for i, p in enumerate(far):
        for d in range(locals_ - 1, 0, -1):
            for there, target in beside(d):
                @pl.when(there)
                def _():
                    own = far_block(me_l, me_n, p)
                    remote(own, own, zraw_send, zraw_recv.at[me_l, i], {"local": target}).start()
    for i, p in enumerate(far):
        for k in range(1, nodes):
            own = far_block(me_l, me_n, p)
            remote(own, own, plane_send, plane_recv.at[i], node_at(k)).start()

    @pl.when(me_r == 0)
    def _():
        pl.semaphore_signal(turn, inc=1, device_id=peer, device_id_type=MESH)

    w_at = 0
    w_rows = []
    for p, (way, at, size, place) in enumerate(pairs):
        for h in range(2):
            pltpu.make_async_copy(
                w_ref.at[pl.ds(h * half + at, size), :], w_buf.at[pl.ds(w_at + h * size, size), :], w_sem.at[p]
            ).start()
        w_rows.append(pl.ds(w_at, 2 * size))
        w_at += 2 * size

    pltpu.make_async_copy(gate_up, gate_up, load_sem).wait()
    gate, up = gate_up[0].astype(F32), gate_up[1].astype(F32)
    sig = jax.nn.sigmoid(gate)
    act = gate * sig
    hidden_buf[...] = act * up
    up_factor[...] = act
    gate_factor[...] = up * sig * (1.0 + gate * (1.0 - sig))

    received(meta.at[0:nodes - 1], meta_recv)
    own_meta = jnp.concatenate([meta[n] for n in range(nodes)], axis=1)
    own_ids, own_rw = own_meta[0:top], own_meta[top:2 * top]
    low = (me_n * exp_group).astype(F32)
    named = [jnp.where(own_ids == low + j, 1.0, 0.0) for j in range(exp_group)]
    hits = [jnp.sum(match, axis=0, keepdims=True) for match in named]
    in_group = jnp.where(sum(hits) > 0, 1.0, 0.0)
    before = earlier_counts(stacked(hits + [in_group]), cohort)
    pick = one_hot(in_group, before[exp_group:exp_group + 1], group_tok).astype(BF16)

    def send_pack(i):
        p = near[i]
        received(nraw.at[0:nodes - 1, :, block(p)], nraw_recv.at[i])
        rows = nraw[:, :, block(p)].reshape(cohort, 2 * pairs[p][2])
        gath[me_l, :, block(p)] = jnp.dot(pick, rows, preferred_element_type=F32).astype(BF16)
        for d in range(locals_ - 1, 0, -1):
            for s, (there, target) in enumerate(((me_l + d < locals_, me_l + d), (me_l >= d, me_l - d))):
                if d > REACH:
                    there = there & (me_r == 0)
                send_to(i, d, s, there, me_l, target, d)

    def onward(d, s):
        return (me_r == 1) & ((me_l + d + 1 < locals_) if s == 0 else (me_l >= d + 1))

    def send_to(i, d, s, there, source, target, hop):
        pack = gath.at[source, :, block(near[i])]
        if REACH <= d < locals_ - 1:
            further = onward(hop, s)

            @pl.when(there & further)
            def _():
                remote(pack, pack, pack_send, relay_recv.at[d - REACH, s, i], {"local": target}).start()

            there = there & jnp.logical_not(further)

        @pl.when(there)
        def _():
            remote(pack, pack, pack_send, pack_recv.at[i], {"local": target}).start()

    def send_cohort_meta():
        weights = [jnp.sum(match * own_rw, axis=0, keepdims=True) for match in named]
        cohort_meta[me_l] = stacked(weights)[0:exp_group]
        for k in range(1, locals_):
            own = cohort_meta.at[me_l]
            remote(own, own, cmeta_send, cmeta_recv, local_at(k)).start()

    def relays(d):
        return [
            ((me_r == 1) & (me_l >= d) & (me_l + 1 < locals_), me_l - d, me_l + 1),
            ((me_r == 1) & (me_l + d < locals_) & (me_l >= 1), me_l + d, me_l - 1),
        ]

    def relay_pack(i, d):
        for s, (there, source, target) in enumerate(relays(d)):
            @pl.when(there)
            def _():
                received(gath.at[source, :, block(near[i])], relay_recv.at[d - REACH, s, i])

            send_to(i, d + 1, s, there, source, target, 1)

    def forward(i, d):
        p = far[i]
        for there, source in beside(d):
            @pl.when(there)
            def _():
                piece = far_block(source, me_n, p)
                received(piece, zraw_recv.at[source, i])
                for target in range(nodes):
                    @pl.when(target != me_n)
                    def _():
                        remote(piece, piece, plane_send, plane_recv.at[i], {"node": target}).start()

    state = {}

    def prepare():
        received(cohort_meta.at[0:locals_ - 1], cmeta_recv)
        total = locals_ * cohort
        weights = jnp.concatenate([cohort_meta[l] for l in range(locals_)], axis=1)
        mine = lax.broadcasted_iota(jnp.int32, (exp_group, total), 0) == me_l // owners
        row_weight = jnp.sum(jnp.where(mine, weights, 0.0), axis=0, keepdims=True)
        member = jnp.where(row_weight > 0, 1.0, 0.0)
        grouped = jnp.where(jnp.sum(weights, axis=0, keepdims=True) > 0, 1.0, 0.0)
        earlier = earlier_counts(stacked([member, grouped]), cohort)
        which = (lax.broadcasted_iota(jnp.int32, (1, total), 1) // cohort).astype(F32)
        slot_hot = one_hot(member, earlier[0:1] + which * capacity, slots)
        pack_hot = one_hot(grouped, earlier[1:2] + which * group_tok, locals_ * group_tok)
        state["far"] = slot_hot.astype(BF16)
        state["near"] = lax.dot_general(
            slot_hot.astype(BF16), pack_hot.astype(BF16),
            (((1,), (1,)), ((), ())), preferred_element_type=F32,
        ).astype(BF16)
        weight = jnp.sum(slot_hot * row_weight, axis=1, keepdims=True)
        state["weight"] = weight
        weighted = (weight * hidden_buf[...]).astype(BF16)
        for way in ways:
            mix[mix_rows(way, 0), :] = contract_rows(state[way], weighted).astype(BF16)
        mix_copy.start()

    ways = ("near", "far")
    mix_half = mix.shape[0] // 2
    mix_copy = remote(mix.at[0:mix_half, :], mix.at[mix_half:2 * mix_half, :], mix_send, mix_recv, peer)

    def mix_rows(way, r):
        start = 0 if way == "near" else locals_ * group_tok
        return pl.ds(r * mix_half + start, locals_ * (group_tok if way == "near" else cohort))

    def half_of(p, r):
        return pl.ds(pl.multiple_of(pairs[p][3] + r * pairs[p][2], 128), pairs[p][2])

    def peer_part(p):
        return pl.ds(pairs[p][3] // 2, pairs[p][2])

    def rows_copy(p):
        w, there = ways.index(pairs[p][0]), half_of(p, 1 - me_r)
        if w == 0:
            return remote(gath.at[:, :, there], near_peer.at[:, :, peer_part(p)], rows_send.at[w], rows_recv.at[w], peer)
        return remote(far_rows.at[:, there], far_peer.at[:, peer_part(p)], rows_send.at[w], rows_recv.at[w], peer)

    relayed = sum(there.astype(jnp.int32) for d in range(REACH, locals_ - 1) for there, _, _ in relays(d))

    def arrived(p):
        if pairs[p][0] == "far":
            received(zraw.at[:, 0:nodes - 1, :, block(p)], plane_recv.at[far.index(p)])
            return
        for count in range(1, locals_):
            @pl.when(locals_ - 1 - relayed == count)
            def _():
                received(gath.at[0:count, :, block(p)], pack_recv.at[near.index(p)])

    def finish(p):
        way, at, size, place = pairs[p]
        arrived(p)
        if way == "far":
            rows = zraw[:, :, :, block(p)].reshape(locals_ * cohort, 2 * size)
            far_rows[:, block(p)] = rows
        else:
            rows = gath[:, :, block(p)].reshape(locals_ * group_tok, 2 * size)
        rows_copy(p).start()
        w_part = w_buf.at[w_rows[p], :]
        pltpu.make_async_copy(w_part, w_part, w_sem.at[p]).wait()
        term = jnp.dot(rows, w_buf[w_rows[p], :], preferred_element_type=F32).astype(BF16)
        return jnp.dot(state[way], term, preferred_element_type=F32)

    def outer(p, fresh):
        way, at, size, place = pairs[p]
        if fresh:
            received(near_peer if way == "near" else far_peer, rows_recv.at[ways.index(way)])
        for t in range(0, size, TILE):
            wide = min(TILE, size - t)
            mine = pl.ds(pl.multiple_of(place + me_r * size + t, 128), wide)
            theirs = pl.ds(place // 2 + t, wide)
            if way == "near":
                pieces = [
                    gath[:, :, mine].reshape(locals_ * group_tok, wide),
                    near_peer[:, :, theirs].reshape(locals_ * group_tok, wide),
                ]
            else:
                pieces = [far_rows[:, mine], far_peer[:, theirs]]
            down_out[pl.ds(at + t, wide), :] = contract_rows(
                jnp.concatenate(pieces, axis=0),
                jnp.concatenate([mix[mix_rows(way, 0), :], mix[mix_rows(way, 1), :]], axis=0),
            ).astype(BF16)

    send_cohort_meta()
    send_pack(0)
    forward(0, 1)
    send_pack(1)
    forward(0, 2)
    forward(0, 3)
    forward(1, 1)
    relay_pack(0, 2)
    forward(1, 2)
    relay_pack(1, 2)
    forward(1, 3)
    prepare()
    order = [near[0], far[0], near[1], far[1]]
    for n, p in enumerate(order):
        product = finish(p)
        if n == 0:
            acc[...] = product
        elif n < len(order) - 1:
            acc[...] += product
    back = acc[...] + product
    shares = jnp.sum(hidden_buf[...] * back, axis=1, keepdims=True)
    share_buf[...] = jnp.broadcast_to(shares, (slots, 128)).astype(BF16).reshape(locals_, capacity, 128)
    for target in range(locals_):
        @pl.when(target != me_l)
        def _():
            remote(share_buf.at[target], back_buf.at[me_l], share_send, share_recv, {"local": target}).start()
    back_buf[me_l] = share_buf[me_l]
    scaled = state["weight"] * back
    ggate_out[...] = (scaled * gate_factor[...]).astype(BF16)
    gup_out[...] = (scaled * up_factor[...]).astype(BF16)
    mix_copy.wait_recv()
    for p in order:
        outer(p, p in (near[0], far[0]))

    sent(meta.at[0:nodes - 1], meta_send)
    sent(nraw.at[0:nodes - 1], raw_send)
    sent(zraw.at[0:locals_ - 1, 0], zraw_send)
    sent(zraw.at[:, 0:nodes - 1], plane_send)
    sent(cohort_meta.at[0:locals_ - 1], cmeta_send)
    pushed = relayed
    for d in range(1, locals_):
        for there in (me_l + d < locals_, me_l >= d):
            if d > REACH:
                there = there & (me_r == 0)
            pushed = pushed + there.astype(jnp.int32)
    for count in range(1, 2 * locals_):
        @pl.when(pushed == count)
        def _():
            for _ in range(count // locals_):
                sent(gath, pack_send)
            if count % locals_:
                sent(gath.at[0:count % locals_], pack_send)

    mix_copy.wait_send()
    sent(near_peer, rows_send.at[0])
    sent(far_peer, rows_send.at[1])
    sent(share_buf.at[0:locals_ - 1], share_send)
    chosen = [one_hot(hits[j], before[j:j + 1], capacity) for j in range(exp_group)]
    received(back_buf.at[0:locals_ - 1], share_recv)
    route = []
    for j in range(exp_group):
        value = jnp.zeros((capacity, 1), F32)
        for o in range(owners):
            value = value + back_buf[j * owners + o, :, 0:1].astype(F32)
        route.append(jnp.sum(chosen[j] * value, axis=0, keepdims=True))
    route_out[...] = stacked(route)[0:exp_group].astype(BF16)


def write_kernel(gate_in, up_in, down_in, route_in, gate_to, up_to, down_to, route_to, sems):
    pairs = ((down_in, down_to), (gate_in, gate_to), (up_in, up_to), (route_in, route_to))
    copies = [pltpu.make_async_copy(src, dst, sems.at[t]) for t, (src, dst) in enumerate(pairs)]
    for copy in copies:
        copy.start()
    for copy in copies:
        copy.wait()


def gathered(nodes, locals_, group_tok, grad_out, expert_ids, route_weights, gate_pre, up_pre, w_down_t):
    tok, width = grad_out.shape
    top = expert_ids.shape[1]
    slots, hs = gate_pre.shape
    owners = H // hs
    exp_group = locals_ // owners
    cohort = nodes * tok
    capacity = slots // locals_
    half = width // 2
    pairs, near_width, far_width = column_pairs(half)
    near_pairs = sum(1 for pair in pairs if pair[0] == "near")
    far_pairs = len(pairs) - near_pairs
    dims = (nodes, locals_, tok, top, width, hs, group_tok, owners)
    dma = pltpu.SemaphoreType.DMA
    hbm = pl.BlockSpec(memory_space=pltpu.HBM)
    shapes = (
        jax.ShapeDtypeStruct((slots, hs), BF16),
        jax.ShapeDtypeStruct((slots, hs), BF16),
        jax.ShapeDtypeStruct((half, hs), BF16),
        jax.ShapeDtypeStruct((exp_group, cohort), BF16),
    )
    results = pl.pallas_call(
        functools.partial(routed_kernel, dims),
        out_shape=shapes,
        in_specs=[hbm] * 6,
        out_specs=tuple([pl.BlockSpec(memory_space=pltpu.VMEM)] * 4),
        scratch_shapes=[
            pltpu.VMEM((2 * locals_ * (group_tok + cohort), hs), BF16),
            pltpu.VMEM((top, tok), jnp.int32),
            pltpu.VMEM((top, tok), BF16),
            pltpu.VMEM((nodes, 2 * top, tok), F32),
            pltpu.VMEM((locals_, exp_group, cohort), F32),
            pltpu.VMEM((nodes, tok, near_width), BF16),
            pltpu.VMEM((locals_, group_tok, near_width), BF16),
            pltpu.VMEM((locals_, nodes, tok, far_width), BF16),
            pltpu.VMEM((locals_ * cohort, far_width), BF16),
            pltpu.VMEM((locals_, group_tok, near_width // 2), BF16),
            pltpu.VMEM((locals_ * cohort, far_width // 2), BF16),
            pltpu.VMEM((width, hs), BF16),
            pltpu.VMEM((2, slots, hs), BF16),
            pltpu.VMEM((slots, hs), F32),
            pltpu.VMEM((slots, hs), F32),
            pltpu.VMEM((slots, hs), F32),
            pltpu.VMEM((slots, hs), F32),
            pltpu.VMEM((locals_, capacity, 128), BF16),
            pltpu.VMEM((locals_, capacity, 128), BF16),
            dma((4,)), dma(()), dma((len(pairs),)),
            dma(()), dma(()), dma(()), dma((near_pairs,)),
            dma(()), dma((locals_, far_pairs)), dma(()), dma((far_pairs,)),
            dma(()), dma((near_pairs,)), dma((max(1, locals_ - 1 - REACH), 2, near_pairs)), dma(()), dma(()),
            dma(()), dma(()), dma((2,)), dma((2,)), dma(()), dma(()), pltpu.SemaphoreType.REGULAR,
        ],
        compiler_params=pltpu.CompilerParams(collective_id=0, has_side_effects=True, **KERNEL_PARAMS),
        name="routed",
    )(*[
        pltpu.with_memory_space_constraint(x, pltpu.HBM)
        for x in (expert_ids.T, route_weights.T, grad_out, gate_pre, up_pre, w_down_t)
    ])
    grad_gate, grad_up, grad_down, grad_route = pl.pallas_call(
        write_kernel,
        out_shape=shapes,
        in_specs=[pl.BlockSpec(memory_space=pl.ANY)] * 4,
        out_specs=tuple([pl.BlockSpec(memory_space=pl.ANY)] * 4),
        scratch_shapes=[dma((4,))],
        compiler_params=pltpu.CompilerParams(vmem_limit_bytes=1024 * 1024),
        name="write",
    )(*results)
    return grad_gate, grad_up, grad_down, grad_route.T


def swapped(block, axis, distance):
    count = lax.axis_size(axis)
    route = []
    for low in range(count):
        high = low | 1 << distance
        if high != low and high < count:
            route += [(low, high), (high, low)]
    return lax.ppermute(block, axis, route)


def outer_term(columns, weighted):
    return lax.dot_general(
        columns, weighted, (((0,), (0,)), ((), ())), preferred_element_type=jnp.float32
    )


def exchanged(grad_out, expert_ids, route_weights, gate_pre, up_pre, w_down_t):
    tok_dev, width = grad_out.shape
    slot_rows, hidden_slice = gate_pre.shape
    node_count = lax.axis_size("node")
    local_count = lax.axis_size("local")
    owners = H // hidden_slice
    exp_group = local_count // owners
    experts = exp_group * node_count
    capacity = slot_rows // local_count
    expert_range = lax.iota(jnp.int32, experts)
    route_hits = expert_ids[:, :, None] == expert_range[None, None, :]
    dense_weights = jnp.sum(
        jnp.where(route_hits, route_weights[:, :, None].astype(jnp.float32), 0.0), axis=1
    ).astype(jnp.bfloat16)
    cohort_grad, cohort_weights = (
        lax.all_gather(grad_out, "node", axis=0, tiled=True),
        lax.all_gather(dense_weights, "node", axis=0, tiled=True),
    )
    group_index = lax.axis_index("node")
    group_weights = lax.dynamic_slice_in_dim(cohort_weights, group_index * exp_group, exp_group, 1)
    routed = (group_weights != 0).astype(jnp.int32)
    position = lax.iota(jnp.int32, routed.shape[0])
    below = (position[:, None] > position[None, :]).astype(jnp.bfloat16)
    earlier = jnp.dot(below, routed.astype(jnp.bfloat16), preferred_element_type=jnp.float32).astype(jnp.int32)
    slot_range = lax.iota(jnp.int32, capacity)
    select = (routed[:, :, None] == 1) & (earlier[:, :, None] == slot_range[None, None, :])
    select_half = select.astype(jnp.bfloat16)
    packed = jnp.einsum(
        "cjs,cd->jsd", select_half, cohort_grad, preferred_element_type=jnp.float32
    ).astype(jnp.bfloat16)
    packed_weights = jnp.einsum(
        "cjs,cj->js", select_half, group_weights, preferred_element_type=jnp.float32
    ).astype(jnp.bfloat16)
    send_grad = jnp.broadcast_to(packed[:, None], (exp_group, owners, capacity, width)).reshape(
        local_count, capacity, width
    )
    send_weights = jnp.broadcast_to(packed_weights[:, None], (exp_group, owners, capacity)).reshape(
        local_count, capacity
    )
    recv_grad, recv_weights = (
        lax.all_to_all(send_grad, "local", split_axis=0, concat_axis=0, tiled=True),
        lax.all_to_all(send_weights, "local", split_axis=0, concat_axis=0, tiled=True),
    )
    cotangent = recv_grad.reshape(slot_rows, width)
    weight = recv_weights.reshape(slot_rows, 1).astype(jnp.float32)
    gate_value = gate_pre.astype(jnp.float32)
    up_value = up_pre.astype(jnp.float32)
    backward = jnp.dot(cotangent, w_down_t, preferred_element_type=jnp.float32)
    sigmoid_gate = jax.nn.sigmoid(gate_value)
    activated = gate_value * sigmoid_gate
    hidden = activated * up_value
    shares = jnp.sum(hidden * backward, axis=1).astype(jnp.bfloat16)
    scaled = weight * backward
    grad_gate_pre = (
        scaled * up_value * sigmoid_gate * (1.0 + gate_value * (1.0 - sigmoid_gate))
    ).astype(jnp.bfloat16)
    grad_up_pre = (scaled * activated).astype(jnp.bfloat16)
    weighted = (weight * hidden).astype(jnp.bfloat16)
    returned = lax.all_to_all(
        shares.reshape(local_count, capacity), "local", split_axis=0, concat_axis=0, tiled=True
    )
    slice_sum = jnp.sum(returned.astype(jnp.float32).reshape(exp_group, owners, capacity), axis=1)
    grad_route = jnp.sum(jnp.where(select, slice_sum[None], 0.0), axis=2).astype(jnp.bfloat16)
    half_width = width // lax.axis_size("rep")
    replica = lax.axis_index("rep")
    own_cols = lax.dynamic_slice_in_dim(cotangent, replica * half_width, half_width, 1)
    peer_cols = lax.dynamic_slice_in_dim(cotangent, (1 - replica) * half_width, half_width, 1)
    got_cols, got_weighted = swapped((peer_cols, weighted), "rep", 0)
    own_term = outer_term(own_cols, weighted).astype(jnp.bfloat16).astype(jnp.float32)
    peer_term = outer_term(got_cols, got_weighted).astype(jnp.bfloat16).astype(jnp.float32)
    grad_down_t = (own_term + peer_term).astype(jnp.bfloat16)
    return (grad_gate_pre, grad_up_pre, grad_down_t, grad_route)


def per_device(grad_out, expert_ids, route_weights, gate_pre, up_pre, w_down_t):
    nodes, locals_ = lax.axis_size("node"), lax.axis_size("local")
    capacity = gate_pre.shape[0] // locals_
    group_tok = grad_out.shape[0] * expert_ids.shape[1] // PER_GROUP
    args = (grad_out, expert_ids, route_weights, gate_pre, up_pre, w_down_t)
    if group_tok > capacity:
        return exchanged(*args)
    return gathered(nodes, locals_, group_tok, *args)


def solution(mesh):
    placed = (
        P(("node", "local", "rep"), None),
        P(("node", "local", "rep"), None),
        P(("node", "local", "rep"), None),
        P("rep", ("node", "local")),
        P("rep", ("node", "local")),
        P(None, ("node", "local")),
    )
    return jax.shard_map(
        per_device,
        mesh=mesh,
        in_specs=placed,
        out_specs=(
            P("rep", ("node", "local")),
            P("rep", ("node", "local")),
            P("rep", ("node", "local")),
            P(("local", "rep"), "node"),
        ),
        check_vma=False,
    )
```

```python
import functools
import jax
import jax.numpy as jnp
from jax import lax
from jax.experimental import pallas as pl
from jax.experimental.pallas import tpu as pltpu
from jax.sharding import PartitionSpec as P

H = 1024
PER_GROUP = 2
PAIRS = (("near", 4), ("far", 4), ("near", 4), ("far", 4))
TILE = 256
REACH = 2
MESH = pl.DeviceIdType.MESH
F32 = jnp.float32
BF16 = jnp.bfloat16
KERNEL_PARAMS = dict(vmem_limit_bytes=40 * 1024 * 1024)


def contract_rows(left, right):
    return lax.dot_general(left, right, (((0,), (0,)), ((), ())), preferred_element_type=F32)


def one_hot(member, row, height):
    places = lax.broadcasted_iota(jnp.int32, (height, member.shape[1]), 0).astype(F32)
    return jnp.where((member > 0) & (row == places), 1.0, 0.0)


def earlier_counts(rows, block):
    count = rows.shape[1]
    above = lax.broadcasted_iota(jnp.int32, (count, count), 0)
    col = lax.broadcasted_iota(jnp.int32, (count, count), 1)
    strict = jnp.where((above < col) & (above // block == col // block), 1.0, 0.0).astype(BF16)
    return jnp.dot(rows.astype(BF16), strict, preferred_element_type=F32)


def stacked(rows):
    lines = lax.broadcasted_iota(jnp.int32, (8, rows[0].shape[1]), 0)
    out = jnp.zeros(lines.shape, F32)
    for place, row in enumerate(rows):
        out = jnp.where(lines == place, row, out)
    return out


def column_pairs(half):
    parts = sum(share for _, share in PAIRS)
    pairs, taken, at = [], {"near": 0, "far": 0}, 0
    for way, share in PAIRS:
        size = half * share // parts
        pairs.append((way, at, size, taken[way]))
        taken[way] += 2 * size
        at += size
    return pairs, taken["near"], taken["far"]


def routed_kernel(
    dims, ids_ref, rw_ref, grad_ref, gate_ref, up_ref, w_ref,
    ggate_out, gup_out, down_out, route_out,
    mix, ids_buf, rw_buf, meta, cohort_meta, nraw, gath, zraw, far_rows, near_peer, far_peer, w_buf, gate_up,
    acc, hidden_buf, gate_factor, up_factor, share_buf, back_buf,
    own_sem, load_sem, w_sem,
    meta_send, meta_recv, raw_send, nraw_recv, zraw_send, zraw_recv, plane_send, plane_recv,
    pack_send, pack_recv, relay_recv, cmeta_send, cmeta_recv,
    mix_send, mix_recv, rows_send, rows_recv, share_send, share_recv, turn,
):
    nodes, locals_, tok, top, width, hs, group_tok, owners = dims
    cohort = nodes * tok
    exp_group = locals_ // owners
    slots = gate_ref.shape[0]
    capacity = slots // locals_
    half = width // 2
    pairs, near_width, far_width = column_pairs(half)
    near = [p for p, pair in enumerate(pairs) if pair[0] == "near"]
    far = [p for p, pair in enumerate(pairs) if pair[0] == "far"]
    me_n, me_l, me_r = lax.axis_index("node"), lax.axis_index("local"), lax.axis_index("rep")
    peer = {"rep": 1 - me_r}

    def node_at(k):
        return {"node": lax.rem(me_n + k, nodes)}

    def local_at(k):
        return {"local": lax.rem(me_l + k, locals_)}

    def remote(src, dst, send, recv, device):
        return pltpu.make_async_remote_copy(
            src_ref=src, dst_ref=dst, send_sem=send, recv_sem=recv,
            device_id=device, device_id_type=MESH,
        )

    def received(ref, sem):
        remote(ref, ref, sem, sem, peer).wait_recv()

    def sent(ref, sem):
        remote(ref, ref, sem, sem, peer).wait_send()

    barrier = pltpu.get_barrier_semaphore()
    for k in range(1, nodes):
        pl.semaphore_signal(barrier, inc=1, device_id=node_at(k), device_id_type=MESH)
    for k in range(1, locals_):
        pl.semaphore_signal(barrier, inc=1, device_id=local_at(k), device_id_type=MESH)
    pl.semaphore_signal(barrier, inc=1, device_id=peer, device_id_type=MESH)

    def block(p):
        return pl.ds(pairs[p][3], 2 * pairs[p][2])

    def part(p):
        return pl.ds(pairs[p][1], pairs[p][2])

    id_copy = pltpu.make_async_copy(ids_ref, ids_buf, own_sem.at[0])
    rw_copy = pltpu.make_async_copy(rw_ref, rw_buf, own_sem.at[1])
    id_copy.start()
    rw_copy.start()
    for p, (way, at, size, place) in enumerate(pairs):
        for h in range(2):
            here = pl.ds(place + h * size, size)
            target = nraw.at[me_n, :, here] if way == "near" else zraw.at[me_l, me_n, :, here]
            pltpu.make_async_copy(
                grad_ref.at[:, pl.ds(h * half + at, size)], target, own_sem.at[2 if way == "near" else 3]
            ).start()
    pltpu.make_async_copy(gate_ref, gate_up.at[0], load_sem).start()
    pltpu.make_async_copy(up_ref, gate_up.at[1], load_sem).start()
    id_copy.wait()
    rw_copy.wait()
    meta[me_n, 0:top, :] = ids_buf[...].astype(F32)
    meta[me_n, top:2 * top, :] = rw_buf[...].astype(F32)
    own_near, own_far = nraw.at[me_n], zraw.at[me_l, me_n]
    pltpu.make_async_copy(own_near, own_near, own_sem.at[2]).wait()
    pltpu.make_async_copy(own_far, own_far, own_sem.at[3]).wait()
    pl.semaphore_wait(barrier, nodes + locals_ - 1)

    for k in range(1, nodes):
        remote(meta.at[me_n], meta.at[me_n], meta_send, meta_recv, node_at(k)).start()

    def beside(d):
        return [(me_l >= d, me_l - d), (me_l + d < locals_, me_l + d)]

    def far_block(l, n, p):
        return zraw.at[l, n, :, block(p)]

    for i, p in enumerate(near):
        for k in range(1, nodes):
            own = nraw.at[me_n, :, block(p)]
            remote(own, own, raw_send, nraw_recv.at[i], node_at(k)).start()
    @pl.when(me_r == 1)
    def _():
        pl.semaphore_wait(turn, 1)

    for i, p in enumerate(far):
        for d in range(locals_ - 1, 0, -1):
            for there, target in beside(d):
                @pl.when(there)
                def _():
                    own = far_block(me_l, me_n, p)
                    remote(own, own, zraw_send, zraw_recv.at[me_l, i], {"local": target}).start()
    def spread(i, source, targets):
        piece = far_block(source, me_n, far[i])
        for target in targets:
            @pl.when(target != me_n)
            def _():
                remote(piece, piece, plane_send, plane_recv.at[i], {"node": target}).start()

    for targets in (range(1), range(1, nodes)):
        for i in range(len(far)):
            spread(i, me_l, targets)

    @pl.when(me_r == 0)
    def _():
        pl.semaphore_signal(turn, inc=1, device_id=peer, device_id_type=MESH)

    w_at = 0
    w_rows = []
    for p, (way, at, size, place) in enumerate(pairs):
        for h in range(2):
            pltpu.make_async_copy(
                w_ref.at[pl.ds(h * half + at, size), :], w_buf.at[pl.ds(w_at + h * size, size), :], w_sem
            ).start()
        w_rows.append(pl.ds(w_at, 2 * size))
        w_at += 2 * size

    pltpu.make_async_copy(gate_up, gate_up, load_sem).wait()
    gate, up = gate_up[0].astype(F32), gate_up[1].astype(F32)
    sig = jax.nn.sigmoid(gate)
    act = gate * sig
    hidden_buf[...] = act * up
    up_factor[...] = act
    gate_factor[...] = up * sig * (1.0 + gate * (1.0 - sig))

    received(meta.at[0:nodes - 1], meta_recv)
    own_meta = jnp.concatenate([meta[n] for n in range(nodes)], axis=1)
    own_ids, own_rw = own_meta[0:top], own_meta[top:2 * top]
    low = (me_n * exp_group).astype(F32)
    named = [jnp.where(own_ids == low + j, 1.0, 0.0) for j in range(exp_group)]
    hits = [jnp.sum(match, axis=0, keepdims=True) for match in named]
    in_group = jnp.where(sum(hits) > 0, 1.0, 0.0)
    before = earlier_counts(stacked(hits + [in_group]), cohort)
    pick = one_hot(in_group, before[exp_group:exp_group + 1], group_tok).astype(BF16)

    def send_pack(i):
        p = near[i]
        received(nraw.at[0:nodes - 1, :, block(p)], nraw_recv.at[i])
        rows = nraw[:, :, block(p)].reshape(cohort, 2 * pairs[p][2])
        gath[me_l, :, block(p)] = jnp.dot(pick, rows, preferred_element_type=F32).astype(BF16)
        for d in range(locals_ - 1, 0, -1):
            for s, (there, target) in enumerate(((me_l + d < locals_, me_l + d), (me_l >= d, me_l - d))):
                if d > REACH:
                    there = there & (me_r == 0)
                send_to(i, d, s, there, me_l, target, d)

    sides = 2 if locals_ > 2 * REACH else 1

    def onward(d, s):
        return (me_r == 1) & ((me_l + d + 1 < locals_) if s == 0 else (me_l >= d + 1))

    def send_to(i, d, s, there, source, target, hop):
        pack = gath.at[source, :, block(near[i])]
        if REACH <= d < locals_ - 1:
            further = onward(hop, s)

            @pl.when(there & further)
            def _():
                remote(pack, pack, pack_send, relay_recv.at[d - REACH, s % sides, i], {"local": target}).start()

            there = there & jnp.logical_not(further)

        @pl.when(there)
        def _():
            remote(pack, pack, pack_send, pack_recv.at[i], {"local": target}).start()

    def send_cohort_meta():
        weights = [jnp.sum(match * own_rw, axis=0, keepdims=True) for match in named]
        cohort_meta[me_l] = stacked(weights)[0:exp_group]
        for k in range(1, locals_):
            own = cohort_meta.at[me_l]
            remote(own, own, cmeta_send, cmeta_recv, local_at(k)).start()

    def relays(d):
        return [
            ((me_r == 1) & (me_l >= d) & (me_l + 1 < locals_), me_l - d, me_l + 1),
            ((me_r == 1) & (me_l + d < locals_) & (me_l >= 1), me_l + d, me_l - 1),
        ]

    def relay_pack(i, d):
        for s, (there, source, target) in enumerate(relays(d)):
            @pl.when(there)
            def _():
                received(gath.at[source, :, block(near[i])], relay_recv.at[d - REACH, s % sides, i])

            send_to(i, d + 1, s, there, source, target, 1)

    def forward(i, d, rest=False):
        for there, source in beside(d):
            @pl.when(there)
            def _():
                if not rest:
                    received(far_block(source, me_n, far[i]), zraw_recv.at[source, i])
                spread(i, source, range(1, nodes) if rest else range(1))

    state = {}

    def prepare():
        received(cohort_meta.at[0:locals_ - 1], cmeta_recv)
        total = locals_ * cohort
        weights = jnp.concatenate([cohort_meta[l] for l in range(locals_)], axis=1)
        mine = lax.broadcasted_iota(jnp.int32, (exp_group, total), 0) == me_l // owners
        row_weight = jnp.sum(jnp.where(mine, weights, 0.0), axis=0, keepdims=True)
        member = jnp.where(row_weight > 0, 1.0, 0.0)
        grouped = jnp.where(jnp.sum(weights, axis=0, keepdims=True) > 0, 1.0, 0.0)
        earlier = earlier_counts(stacked([member, grouped]), cohort)
        which = (lax.broadcasted_iota(jnp.int32, (1, total), 1) // cohort).astype(F32)
        slot_hot = one_hot(member, earlier[0:1] + which * capacity, slots)
        pack_hot = one_hot(grouped, earlier[1:2] + which * group_tok, locals_ * group_tok)
        state["far"] = slot_hot.astype(BF16)
        state["near"] = lax.dot_general(
            slot_hot.astype(BF16), pack_hot.astype(BF16),
            (((1,), (1,)), ((), ())), preferred_element_type=F32,
        ).astype(BF16)
        weight = jnp.sum(slot_hot * row_weight, axis=1, keepdims=True)
        state["weight"] = weight
        weighted = (weight * hidden_buf[...]).astype(BF16)
        for way in ways:
            mix[mix_rows(way, 0), :] = contract_rows(state[way], weighted).astype(BF16)
        mix_copy.start()

    ways = ("near", "far")
    mix_half = mix.shape[0] // 2
    mix_copy = remote(mix.at[0:mix_half, :], mix.at[mix_half:2 * mix_half, :], mix_send, mix_recv, peer)

    def mix_rows(way, r):
        start = 0 if way == "near" else locals_ * group_tok
        return pl.ds(r * mix_half + start, locals_ * (group_tok if way == "near" else cohort))

    def half_of(p, r):
        return pl.ds(pl.multiple_of(pairs[p][3] + r * pairs[p][2], 128), pairs[p][2])

    def peer_part(p):
        return pl.ds(pairs[p][3] // 2, pairs[p][2])

    def rows_copy(p):
        w, there = ways.index(pairs[p][0]), half_of(p, 1 - me_r)
        if w == 0:
            return remote(gath.at[:, :, there], near_peer.at[:, :, peer_part(p)], rows_send.at[w], rows_recv.at[w], peer)
        return remote(far_rows.at[:, there], far_peer.at[:, peer_part(p)], rows_send.at[w], rows_recv.at[w], peer)

    relayed = sum(there.astype(jnp.int32) for d in range(REACH, locals_ - 1) for there, _, _ in relays(d))

    def arrived(p):
        if pairs[p][0] == "far":
            received(zraw.at[:, 0:nodes - 1, :, block(p)], plane_recv.at[far.index(p)])
            return
        for count in range(1, locals_):
            @pl.when(locals_ - 1 - relayed == count)
            def _():
                received(gath.at[0:count, :, block(p)], pack_recv.at[near.index(p)])

    def multiplied(p):
        way, at, size, place = pairs[p]
        if way == "far":
            rows = zraw[:, :, :, block(p)].reshape(locals_ * cohort, 2 * size)
            far_rows[:, block(p)] = rows
        else:
            rows = gath[:, :, block(p)].reshape(locals_ * group_tok, 2 * size)
        return jnp.dot(rows, w_buf[w_rows[p], :], preferred_element_type=F32).astype(BF16)

    def selected(p, product):
        return jnp.dot(state[pairs[p][0]], product, preferred_element_type=F32)

    def outer(p, fresh):
        way, at, size, place = pairs[p]
        if fresh:
            received(near_peer if way == "near" else far_peer, rows_recv.at[ways.index(way)])
        for t in range(0, size, TILE):
            wide = min(TILE, size - t)
            mine = pl.ds(pl.multiple_of(place + me_r * size + t, 128), wide)
            theirs = pl.ds(place // 2 + t, wide)
            if way == "near":
                pieces = [
                    gath[:, :, mine].reshape(locals_ * group_tok, wide),
                    near_peer[:, :, theirs].reshape(locals_ * group_tok, wide),
                ]
            else:
                pieces = [far_rows[:, mine], far_peer[:, theirs]]
            down_out[pl.ds(at + t, wide), :] = contract_rows(
                jnp.concatenate(pieces, axis=0),
                jnp.concatenate([mix[mix_rows(way, 0), :], mix[mix_rows(way, 1), :]], axis=0),
            ).astype(BF16)

    send_cohort_meta()
    send_pack(0)
    forward(0, 1)
    forward(0, 1, True)
    send_pack(1)
    forward(0, 2)
    forward(0, 3)
    forward(1, 1)
    forward(1, 2)
    forward(1, 3)
    forward(0, 2, True)
    forward(0, 3, True)
    forward(1, 1, True)
    forward(1, 2, True)
    forward(1, 3, True)
    relay_pack(0, 2)
    relay_pack(1, 2)
    prepare()
    order = [near[0], far[0], far[1], near[1]]
    stages = [[p] for p in order]
    pltpu.make_async_copy(w_buf, w_buf, w_sem).wait()
    back, waiting = None, []
    for stage in stages:
        for p in stage:
            arrived(p)
        fresh = [(p, multiplied(p)) for p in stage]
        for p, product in waiting:
            back = selected(p, product) if back is None else back + selected(p, product)
        if stage is not stages[-1] and back is not None:
            acc[...] = back
            back = acc[...]
        for p in stage:
            rows_copy(p).start()
        waiting = fresh
    for p, product in waiting:
        back = back + selected(p, product)
    shares = jnp.sum(hidden_buf[...] * back, axis=1, keepdims=True)
    share_buf[...] = jnp.broadcast_to(shares, (slots, 128)).astype(BF16).reshape(locals_, capacity, 128)
    for target in range(locals_):
        @pl.when(target != me_l)
        def _():
            remote(share_buf.at[target], back_buf.at[me_l], share_send, share_recv, {"local": target}).start()
    back_buf[me_l] = share_buf[me_l]
    scaled = state["weight"] * back
    ggate_out[...] = (scaled * gate_factor[...]).astype(BF16)
    gup_out[...] = (scaled * up_factor[...]).astype(BF16)
    mix_copy.wait_recv()
    for p in order:
        outer(p, p in (near[0], far[0]))

    sent(meta.at[0:nodes - 1], meta_send)
    sent(nraw.at[0:nodes - 1], raw_send)
    sent(zraw.at[0:locals_ - 1, 0], zraw_send)
    sent(zraw.at[:, 0:nodes - 1], plane_send)
    sent(cohort_meta.at[0:locals_ - 1], cmeta_send)
    pushed = relayed
    for d in range(1, locals_):
        for there in (me_l + d < locals_, me_l >= d):
            if d > REACH:
                there = there & (me_r == 0)
            pushed = pushed + there.astype(jnp.int32)
    for count in range(1, 2 * locals_):
        @pl.when(pushed == count)
        def _():
            for _ in range(count // locals_):
                sent(gath, pack_send)
            if count % locals_:
                sent(gath.at[0:count % locals_], pack_send)

    mix_copy.wait_send()
    sent(near_peer, rows_send.at[0])
    sent(far_peer, rows_send.at[1])
    sent(share_buf.at[0:locals_ - 1], share_send)
    chosen = [one_hot(hits[j], before[j:j + 1], capacity) for j in range(exp_group)]
    received(back_buf.at[0:locals_ - 1], share_recv)
    route = []
    for j in range(exp_group):
        value = jnp.zeros((capacity, 1), F32)
        for o in range(owners):
            value = value + back_buf[j * owners + o, :, 0:1].astype(F32)
        route.append(jnp.sum(chosen[j] * value, axis=0, keepdims=True))
    route_out[...] = stacked(route)[0:exp_group].astype(BF16)


def write_kernel(gate_in, up_in, down_in, route_in, gate_to, up_to, down_to, route_to, sems):
    pairs = ((down_in, down_to), (gate_in, gate_to), (up_in, up_to), (route_in, route_to))
    copies = [pltpu.make_async_copy(src, dst, sems.at[t]) for t, (src, dst) in enumerate(pairs)]
    for copy in copies:
        copy.start()
    for copy in copies:
        copy.wait()


def gathered(nodes, locals_, group_tok, grad_out, expert_ids, route_weights, gate_pre, up_pre, w_down_t):
    tok, width = grad_out.shape
    top = expert_ids.shape[1]
    slots, hs = gate_pre.shape
    owners = H // hs
    exp_group = locals_ // owners
    cohort = nodes * tok
    capacity = slots // locals_
    half = width // 2
    pairs, near_width, far_width = column_pairs(half)
    near_pairs = sum(1 for pair in pairs if pair[0] == "near")
    far_pairs = len(pairs) - near_pairs
    dims = (nodes, locals_, tok, top, width, hs, group_tok, owners)
    dma = pltpu.SemaphoreType.DMA
    hbm = pl.BlockSpec(memory_space=pltpu.HBM)
    shapes = (
        jax.ShapeDtypeStruct((slots, hs), BF16),
        jax.ShapeDtypeStruct((slots, hs), BF16),
        jax.ShapeDtypeStruct((half, hs), BF16),
        jax.ShapeDtypeStruct((exp_group, cohort), BF16),
    )
    results = pl.pallas_call(
        functools.partial(routed_kernel, dims),
        out_shape=shapes,
        in_specs=[hbm] * 6,
        out_specs=tuple([pl.BlockSpec(memory_space=pltpu.VMEM)] * 4),
        scratch_shapes=[
            pltpu.VMEM((2 * locals_ * (group_tok + cohort), hs), BF16),
            pltpu.VMEM((top, tok), jnp.int32),
            pltpu.VMEM((top, tok), BF16),
            pltpu.VMEM((nodes, 2 * top, tok), F32),
            pltpu.VMEM((locals_, exp_group, cohort), F32),
            pltpu.VMEM((nodes, tok, near_width), BF16),
            pltpu.VMEM((locals_, group_tok, near_width), BF16),
            pltpu.VMEM((locals_, nodes, tok, far_width), BF16),
            pltpu.VMEM((locals_ * cohort, far_width), BF16),
            pltpu.VMEM((locals_, group_tok, near_width // 2), BF16),
            pltpu.VMEM((locals_ * cohort, far_width // 2), BF16),
            pltpu.VMEM((width, hs), BF16),
            pltpu.VMEM((2, slots, hs), BF16),
            pltpu.VMEM((slots, hs), F32),
            pltpu.VMEM((slots, hs), F32),
            pltpu.VMEM((slots, hs), F32),
            pltpu.VMEM((slots, hs), F32),
            pltpu.VMEM((locals_, capacity, 128), BF16),
            pltpu.VMEM((locals_, capacity, 128), BF16),
            dma((4,)), dma(()), dma(()),
            dma(()), dma(()), dma(()), dma((near_pairs,)),
            dma(()), dma((locals_, far_pairs)), dma(()), dma((far_pairs,)),
            dma(()), dma((near_pairs,)), dma((max(1, locals_ - 1 - REACH), 2 if locals_ > 2 * REACH else 1, near_pairs)), dma(()), dma(()),
            dma(()), dma(()), dma((2,)), dma((2,)), dma(()), dma(()), pltpu.SemaphoreType.REGULAR,
        ],
        compiler_params=pltpu.CompilerParams(collective_id=0, has_side_effects=True, **KERNEL_PARAMS),
        name="routed",
    )(*[
        pltpu.with_memory_space_constraint(x, pltpu.HBM)
        for x in (expert_ids.T, route_weights.T, grad_out, gate_pre, up_pre, w_down_t)
    ])
    grad_gate, grad_up, grad_down, grad_route = pl.pallas_call(
        write_kernel,
        out_shape=shapes,
        in_specs=[pl.BlockSpec(memory_space=pl.ANY)] * 4,
        out_specs=tuple([pl.BlockSpec(memory_space=pl.ANY)] * 4),
        scratch_shapes=[dma((4,))],
        compiler_params=pltpu.CompilerParams(vmem_limit_bytes=1024 * 1024),
        name="write",
    )(*results)
    return grad_gate, grad_up, grad_down, grad_route.T


def swapped(block, axis, distance):
    count = lax.axis_size(axis)
    route = []
    for low in range(count):
        high = low | 1 << distance
        if high != low and high < count:
            route += [(low, high), (high, low)]
    return lax.ppermute(block, axis, route)


def outer_term(columns, weighted):
    return lax.dot_general(
        columns, weighted, (((0,), (0,)), ((), ())), preferred_element_type=jnp.float32
    )


def exchanged(grad_out, expert_ids, route_weights, gate_pre, up_pre, w_down_t):
    tok_dev, width = grad_out.shape
    slot_rows, hidden_slice = gate_pre.shape
    node_count = lax.axis_size("node")
    local_count = lax.axis_size("local")
    owners = H // hidden_slice
    exp_group = local_count // owners
    experts = exp_group * node_count
    capacity = slot_rows // local_count
    expert_range = lax.iota(jnp.int32, experts)
    route_hits = expert_ids[:, :, None] == expert_range[None, None, :]
    dense_weights = jnp.sum(
        jnp.where(route_hits, route_weights[:, :, None].astype(jnp.float32), 0.0), axis=1
    ).astype(jnp.bfloat16)
    cohort_grad, cohort_weights = (
        lax.all_gather(grad_out, "node", axis=0, tiled=True),
        lax.all_gather(dense_weights, "node", axis=0, tiled=True),
    )
    group_index = lax.axis_index("node")
    group_weights = lax.dynamic_slice_in_dim(cohort_weights, group_index * exp_group, exp_group, 1)
    routed = (group_weights != 0).astype(jnp.int32)
    position = lax.iota(jnp.int32, routed.shape[0])
    below = (position[:, None] > position[None, :]).astype(jnp.bfloat16)
    earlier = jnp.dot(below, routed.astype(jnp.bfloat16), preferred_element_type=jnp.float32).astype(jnp.int32)
    slot_range = lax.iota(jnp.int32, capacity)
    select = (routed[:, :, None] == 1) & (earlier[:, :, None] == slot_range[None, None, :])
    select_half = select.astype(jnp.bfloat16)
    packed = jnp.einsum(
        "cjs,cd->jsd", select_half, cohort_grad, preferred_element_type=jnp.float32
    ).astype(jnp.bfloat16)
    packed_weights = jnp.einsum(
        "cjs,cj->js", select_half, group_weights, preferred_element_type=jnp.float32
    ).astype(jnp.bfloat16)
    send_grad = jnp.broadcast_to(packed[:, None], (exp_group, owners, capacity, width)).reshape(
        local_count, capacity, width
    )
    send_weights = jnp.broadcast_to(packed_weights[:, None], (exp_group, owners, capacity)).reshape(
        local_count, capacity
    )
    recv_grad, recv_weights = (
        lax.all_to_all(send_grad, "local", split_axis=0, concat_axis=0, tiled=True),
        lax.all_to_all(send_weights, "local", split_axis=0, concat_axis=0, tiled=True),
    )
    cotangent = recv_grad.reshape(slot_rows, width)
    weight = recv_weights.reshape(slot_rows, 1).astype(jnp.float32)
    gate_value = gate_pre.astype(jnp.float32)
    up_value = up_pre.astype(jnp.float32)
    backward = jnp.dot(cotangent, w_down_t, preferred_element_type=jnp.float32)
    sigmoid_gate = jax.nn.sigmoid(gate_value)
    activated = gate_value * sigmoid_gate
    hidden = activated * up_value
    shares = jnp.sum(hidden * backward, axis=1).astype(jnp.bfloat16)
    scaled = weight * backward
    grad_gate_pre = (
        scaled * up_value * sigmoid_gate * (1.0 + gate_value * (1.0 - sigmoid_gate))
    ).astype(jnp.bfloat16)
    grad_up_pre = (scaled * activated).astype(jnp.bfloat16)
    weighted = (weight * hidden).astype(jnp.bfloat16)
    returned = lax.all_to_all(
        shares.reshape(local_count, capacity), "local", split_axis=0, concat_axis=0, tiled=True
    )
    slice_sum = jnp.sum(returned.astype(jnp.float32).reshape(exp_group, owners, capacity), axis=1)
    grad_route = jnp.sum(jnp.where(select, slice_sum[None], 0.0), axis=2).astype(jnp.bfloat16)
    half_width = width // lax.axis_size("rep")
    replica = lax.axis_index("rep")
    own_cols = lax.dynamic_slice_in_dim(cotangent, replica * half_width, half_width, 1)
    peer_cols = lax.dynamic_slice_in_dim(cotangent, (1 - replica) * half_width, half_width, 1)
    got_cols, got_weighted = swapped((peer_cols, weighted), "rep", 0)
    own_term = outer_term(own_cols, weighted).astype(jnp.bfloat16).astype(jnp.float32)
    peer_term = outer_term(got_cols, got_weighted).astype(jnp.bfloat16).astype(jnp.float32)
    grad_down_t = (own_term + peer_term).astype(jnp.bfloat16)
    return (grad_gate_pre, grad_up_pre, grad_down_t, grad_route)


def per_device(grad_out, expert_ids, route_weights, gate_pre, up_pre, w_down_t):
    nodes, locals_ = lax.axis_size("node"), lax.axis_size("local")
    capacity = gate_pre.shape[0] // locals_
    group_tok = grad_out.shape[0] * expert_ids.shape[1] // PER_GROUP
    args = (grad_out, expert_ids, route_weights, gate_pre, up_pre, w_down_t)
    if group_tok > capacity:
        return exchanged(*args)
    return gathered(nodes, locals_, group_tok, *args)


def solution(mesh):
    placed = (
        P(("node", "local", "rep"), None),
        P(("node", "local", "rep"), None),
        P(("node", "local", "rep"), None),
        P("rep", ("node", "local")),
        P("rep", ("node", "local")),
        P(None, ("node", "local")),
    )
    return jax.shard_map(
        per_device,
        mesh=mesh,
        in_specs=placed,
        out_specs=(
            P("rep", ("node", "local")),
            P("rep", ("node", "local")),
            P("rep", ("node", "local")),
            P(("local", "rep"), "node"),
        ),
        check_vma=False,
    )
```

```python
import functools
import jax
import jax.numpy as jnp
from jax import lax
from jax.experimental import pallas as pl
from jax.experimental.pallas import tpu as pltpu
from jax.sharding import PartitionSpec as P

H = 1024
PER_GROUP = 2
PAIRS = (("near", 4), ("far", 4), ("near", 4), ("far", 4))
TILE = 256
REACH = 2
MESH = pl.DeviceIdType.MESH
F32 = jnp.float32
BF16 = jnp.bfloat16
KERNEL_PARAMS = dict(vmem_limit_bytes=40 * 1024 * 1024)


def contract_rows(left, right):
    return lax.dot_general(left, right, (((0,), (0,)), ((), ())), preferred_element_type=F32)


def one_hot(member, row, height):
    places = lax.broadcasted_iota(jnp.int32, (height, member.shape[1]), 0).astype(F32)
    return jnp.where((member > 0) & (row == places), 1.0, 0.0)


def earlier_counts(rows, block):
    count = rows.shape[1]
    above = lax.broadcasted_iota(jnp.int32, (count, count), 0)
    col = lax.broadcasted_iota(jnp.int32, (count, count), 1)
    strict = jnp.where((above < col) & (above // block == col // block), 1.0, 0.0).astype(BF16)
    return jnp.dot(rows.astype(BF16), strict, preferred_element_type=F32)


def stacked(rows):
    lines = lax.broadcasted_iota(jnp.int32, (8, rows[0].shape[1]), 0)
    out = jnp.zeros(lines.shape, F32)
    for place, row in enumerate(rows):
        out = jnp.where(lines == place, row, out)
    return out


def column_pairs(half):
    parts = sum(share for _, share in PAIRS)
    pairs, taken, at = [], {"near": 0, "far": 0}, 0
    for way, share in PAIRS:
        size = half * share // parts
        pairs.append((way, at, size, taken[way]))
        taken[way] += 2 * size
        at += size
    return pairs, taken["near"], taken["far"]


def routed_kernel(
    dims, ids_ref, rw_ref, grad_ref, gate_ref, up_ref, w_ref,
    ggate_out, gup_out, down_out, route_out,
    mix, ids_buf, rw_buf, meta, cohort_meta, nraw, gath, zraw, far_rows, near_peer, far_peer, w_buf, gate_up,
    acc, hidden_buf, gate_factor, up_factor, share_buf, back_buf,
    own_sem, load_sem, w_sem,
    meta_send, meta_recv, raw_send, nraw_recv, zraw_send, zraw_recv, plane_send, plane_recv, hand_recv, own_recv,
    pack_send, pack_recv, relay_recv, cmeta_send, cmeta_recv,
    mix_send, mix_recv, rows_send, rows_recv, share_send, share_recv, turn,
):
    nodes, locals_, tok, top, width, hs, group_tok, owners = dims
    cohort = nodes * tok
    exp_group = locals_ // owners
    slots = gate_ref.shape[0]
    capacity = slots // locals_
    half = width // 2
    pairs, near_width, far_width = column_pairs(half)
    near = [p for p, pair in enumerate(pairs) if pair[0] == "near"]
    far = [p for p, pair in enumerate(pairs) if pair[0] == "far"]
    me_n, me_l, me_r = lax.axis_index("node"), lax.axis_index("local"), lax.axis_index("rep")
    peer = {"rep": 1 - me_r}

    def node_at(k):
        return {"node": lax.rem(me_n + k, nodes)}

    def local_at(k):
        return {"local": lax.rem(me_l + k, locals_)}

    def remote(src, dst, send, recv, device):
        return pltpu.make_async_remote_copy(
            src_ref=src, dst_ref=dst, send_sem=send, recv_sem=recv,
            device_id=device, device_id_type=MESH,
        )

    def received(ref, sem):
        remote(ref, ref, sem, sem, peer).wait_recv()

    def sent(ref, sem):
        remote(ref, ref, sem, sem, peer).wait_send()

    barrier = pltpu.get_barrier_semaphore()
    for k in range(1, nodes):
        pl.semaphore_signal(barrier, inc=1, device_id=node_at(k), device_id_type=MESH)
    for k in range(1, locals_):
        pl.semaphore_signal(barrier, inc=1, device_id=local_at(k), device_id_type=MESH)
    pl.semaphore_signal(barrier, inc=1, device_id=peer, device_id_type=MESH)

    def block(p):
        return pl.ds(pairs[p][3], 2 * pairs[p][2])

    def part(p):
        return pl.ds(pairs[p][1], pairs[p][2])

    id_copy = pltpu.make_async_copy(ids_ref, ids_buf, own_sem.at[0])
    rw_copy = pltpu.make_async_copy(rw_ref, rw_buf, own_sem.at[1])
    id_copy.start()
    rw_copy.start()
    for p, (way, at, size, place) in enumerate(pairs):
        for h in range(2):
            here = pl.ds(place + h * size, size)
            target = nraw.at[me_n, :, here] if way == "near" else zraw.at[me_l, me_n, :, here]
            pltpu.make_async_copy(
                grad_ref.at[:, pl.ds(h * half + at, size)], target, own_sem.at[2 if way == "near" else 3]
            ).start()
    pltpu.make_async_copy(gate_ref, gate_up.at[0], load_sem).start()
    pltpu.make_async_copy(up_ref, gate_up.at[1], load_sem).start()
    id_copy.wait()
    rw_copy.wait()
    meta[me_n, 0:top, :] = ids_buf[...].astype(F32)
    meta[me_n, top:2 * top, :] = rw_buf[...].astype(F32)
    own_near, own_far = nraw.at[me_n], zraw.at[me_l, me_n]
    pltpu.make_async_copy(own_near, own_near, own_sem.at[2]).wait()
    pltpu.make_async_copy(own_far, own_far, own_sem.at[3]).wait()
    pl.semaphore_wait(barrier, nodes + locals_ - 1)

    for k in range(1, nodes):
        remote(meta.at[me_n], meta.at[me_n], meta_send, meta_recv, node_at(k)).start()

    def beside(d):
        return [(me_l >= d, me_l - d), (me_l + d < locals_, me_l + d)]

    def far_block(l, n, p):
        return zraw.at[l, n, :, block(p)]

    for i, p in enumerate(near):
        for k in range(1, nodes):
            own = nraw.at[me_n, :, block(p)]
            remote(own, own, raw_send, nraw_recv.at[i], node_at(k)).start()
    @pl.when(me_r == 1)
    def _():
        pl.semaphore_wait(turn, 1)

    for i, p in enumerate(far):
        for d in range(locals_ - 1, 0, -1):
            for there, target in beside(d):
                @pl.when(there)
                def _():
                    own = far_block(me_l, me_n, p)
                    remote(own, own, zraw_send, zraw_recv.at[me_l, i], {"local": target}).start()
    def spread(i, source, targets):
        piece = far_block(source, me_n, far[i])
        for target in targets:
            @pl.when(target != me_n)
            def _():
                remote(piece, piece, plane_send, plane_recv.at[i], {"node": target}).start()

    square = nodes == 4
    beside_me = (me_n + 1 - 2 * lax.rem(me_n, 2), lax.rem(me_n + 2, 4))

    def hand(i):
        if square:
            piece = far_block(me_l, beside_me[i % 2], far[i])
            received(piece, hand_recv.at[i])
            remote(piece, piece, plane_send, own_recv.at[i], {"node": beside_me[1 - i % 2]}).start()

    for i in range(len(far)):
        own = far_block(me_l, me_n, far[i])
        if square:
            remote(own, own, plane_send, hand_recv.at[i], {"node": beside_me[i % 2]}).start()
            remote(own, own, plane_send, own_recv.at[i], {"node": beside_me[1 - i % 2]}).start()
        else:
            for k in range(1, nodes):
                remote(own, own, plane_send, own_recv.at[i], node_at(k)).start()

    @pl.when(me_r == 0)
    def _():
        pl.semaphore_signal(turn, inc=1, device_id=peer, device_id_type=MESH)

    w_at = 0
    w_rows = []
    for p, (way, at, size, place) in enumerate(pairs):
        for h in range(2):
            pltpu.make_async_copy(
                w_ref.at[pl.ds(h * half + at, size), :], w_buf.at[pl.ds(w_at + h * size, size), :], w_sem
            ).start()
        w_rows.append(pl.ds(w_at, 2 * size))
        w_at += 2 * size

    pltpu.make_async_copy(gate_up, gate_up, load_sem).wait()
    gate, up = gate_up[0].astype(F32), gate_up[1].astype(F32)
    sig = jax.nn.sigmoid(gate)
    act = gate * sig
    hidden_buf[...] = act * up
    up_factor[...] = act
    gate_factor[...] = up * sig * (1.0 + gate * (1.0 - sig))

    received(meta.at[0:nodes - 1], meta_recv)
    own_meta = jnp.concatenate([meta[n] for n in range(nodes)], axis=1)
    own_ids, own_rw = own_meta[0:top], own_meta[top:2 * top]
    low = (me_n * exp_group).astype(F32)
    named = [jnp.where(own_ids == low + j, 1.0, 0.0) for j in range(exp_group)]
    hits = [jnp.sum(match, axis=0, keepdims=True) for match in named]
    in_group = jnp.where(sum(hits) > 0, 1.0, 0.0)
    before = earlier_counts(stacked(hits + [in_group]), cohort)
    pick = one_hot(in_group, before[exp_group:exp_group + 1], group_tok).astype(BF16)

    def send_pack(i):
        p = near[i]
        received(nraw.at[0:nodes - 1, :, block(p)], nraw_recv.at[i])
        rows = nraw[:, :, block(p)].reshape(cohort, 2 * pairs[p][2])
        gath[me_l, :, block(p)] = jnp.dot(pick, rows, preferred_element_type=F32).astype(BF16)
        for d in range(locals_ - 1, 0, -1):
            for s, (there, target) in enumerate(((me_l + d < locals_, me_l + d), (me_l >= d, me_l - d))):
                if d > REACH:
                    there = there & (me_r == 0)
                send_to(i, d, s, there, me_l, target, d)

    sides = 2 if locals_ > 2 * REACH else 1

    def onward(d, s):
        return (me_r == 1) & ((me_l + d + 1 < locals_) if s == 0 else (me_l >= d + 1))

    def send_to(i, d, s, there, source, target, hop):
        pack = gath.at[source, :, block(near[i])]
        if REACH <= d < locals_ - 1:
            further = onward(hop, s)

            @pl.when(there & further)
            def _():
                remote(pack, pack, pack_send, relay_recv.at[d - REACH, s % sides, i], {"local": target}).start()

            there = there & jnp.logical_not(further)

        @pl.when(there)
        def _():
            remote(pack, pack, pack_send, pack_recv.at[i], {"local": target}).start()

    def send_cohort_meta():
        weights = [jnp.sum(match * own_rw, axis=0, keepdims=True) for match in named]
        cohort_meta[me_l] = stacked(weights)[0:exp_group]
        for k in range(1, locals_):
            own = cohort_meta.at[me_l]
            remote(own, own, cmeta_send, cmeta_recv, local_at(k)).start()

    def relays(d):
        return [
            ((me_r == 1) & (me_l >= d) & (me_l + 1 < locals_), me_l - d, me_l + 1),
            ((me_r == 1) & (me_l + d < locals_) & (me_l >= 1), me_l + d, me_l - 1),
        ]

    def relay_pack(i, d):
        for s, (there, source, target) in enumerate(relays(d)):
            @pl.when(there)
            def _():
                received(gath.at[source, :, block(near[i])], relay_recv.at[d - REACH, s % sides, i])

            send_to(i, d + 1, s, there, source, target, 1)

    def forward(i, d, rest=False):
        for there, source in beside(d):
            @pl.when(there)
            def _():
                if not rest:
                    received(far_block(source, me_n, far[i]), zraw_recv.at[source, i])
                spread(i, source, range(1, nodes) if rest else range(1))

    state = {}

    def prepare():
        received(cohort_meta.at[0:locals_ - 1], cmeta_recv)
        total = locals_ * cohort
        weights = jnp.concatenate([cohort_meta[l] for l in range(locals_)], axis=1)
        mine = lax.broadcasted_iota(jnp.int32, (exp_group, total), 0) == me_l // owners
        row_weight = jnp.sum(jnp.where(mine, weights, 0.0), axis=0, keepdims=True)
        member = jnp.where(row_weight > 0, 1.0, 0.0)
        grouped = jnp.where(jnp.sum(weights, axis=0, keepdims=True) > 0, 1.0, 0.0)
        earlier = earlier_counts(stacked([member, grouped]), cohort)
        which = (lax.broadcasted_iota(jnp.int32, (1, total), 1) // cohort).astype(F32)
        slot_hot = one_hot(member, earlier[0:1] + which * capacity, slots)
        pack_hot = one_hot(grouped, earlier[1:2] + which * group_tok, locals_ * group_tok)
        state["far"] = slot_hot.astype(BF16)
        state["near"] = lax.dot_general(
            slot_hot.astype(BF16), pack_hot.astype(BF16),
            (((1,), (1,)), ((), ())), preferred_element_type=F32,
        ).astype(BF16)
        weight = jnp.sum(slot_hot * row_weight, axis=1, keepdims=True)
        state["weight"] = weight
        weighted = (weight * hidden_buf[...]).astype(BF16)
        for way in ways:
            mix[mix_rows(way, 0), :] = contract_rows(state[way], weighted).astype(BF16)
        mix_copy.start()

    ways = ("near", "far")
    mix_half = mix.shape[0] // 2
    mix_copy = remote(mix.at[0:mix_half, :], mix.at[mix_half:2 * mix_half, :], mix_send, mix_recv, peer)

    def mix_rows(way, r):
        start = 0 if way == "near" else locals_ * group_tok
        return pl.ds(r * mix_half + start, locals_ * (group_tok if way == "near" else cohort))

    def half_of(p, r):
        return pl.ds(pl.multiple_of(pairs[p][3] + r * pairs[p][2], 128), pairs[p][2])

    def peer_part(p):
        return pl.ds(pairs[p][3] // 2, pairs[p][2])

    def rows_copy(p):
        w, there = ways.index(pairs[p][0]), half_of(p, 1 - me_r)
        if w == 0:
            return remote(gath.at[:, :, there], near_peer.at[:, :, peer_part(p)], rows_send.at[w], rows_recv.at[w], peer)
        return remote(far_rows.at[:, there], far_peer.at[:, peer_part(p)], rows_send.at[w], rows_recv.at[w], peer)

    relayed = sum(there.astype(jnp.int32) for d in range(REACH, locals_ - 1) for there, _, _ in relays(d))

    def arrived(p):
        if pairs[p][0] == "far":
            i = far.index(p)
            received(zraw.at[me_l, 0:nodes - 1 - square, :, block(p)], own_recv.at[i])
            received(zraw.at[0:locals_ - 1, 0:nodes - 1, :, block(p)], plane_recv.at[i])
            return
        for count in range(1, locals_):
            @pl.when(locals_ - 1 - relayed == count)
            def _():
                received(gath.at[0:count, :, block(p)], pack_recv.at[near.index(p)])

    def multiplied(p):
        way, at, size, place = pairs[p]
        if way == "far":
            rows = zraw[:, :, :, block(p)].reshape(locals_ * cohort, 2 * size)
            far_rows[:, block(p)] = rows
        else:
            rows = gath[:, :, block(p)].reshape(locals_ * group_tok, 2 * size)
        return jnp.dot(rows, w_buf[w_rows[p], :], preferred_element_type=F32).astype(BF16)

    def selected(p, product):
        return jnp.dot(state[pairs[p][0]], product, preferred_element_type=F32)

    def outer(p, fresh):
        way, at, size, place = pairs[p]
        if fresh:
            received(near_peer if way == "near" else far_peer, rows_recv.at[ways.index(way)])
        for t in range(0, size, TILE):
            wide = min(TILE, size - t)
            mine = pl.ds(pl.multiple_of(place + me_r * size + t, 128), wide)
            theirs = pl.ds(place // 2 + t, wide)
            if way == "near":
                pieces = [
                    gath[:, :, mine].reshape(locals_ * group_tok, wide),
                    near_peer[:, :, theirs].reshape(locals_ * group_tok, wide),
                ]
            else:
                pieces = [far_rows[:, mine], far_peer[:, theirs]]
            down_out[pl.ds(at + t, wide), :] = contract_rows(
                jnp.concatenate(pieces, axis=0),
                jnp.concatenate([mix[mix_rows(way, 0), :], mix[mix_rows(way, 1), :]], axis=0),
            ).astype(BF16)

    send_cohort_meta()
    send_pack(0)
    forward(0, 1)
    forward(0, 1, True)
    hand(0)
    send_pack(1)
    hand(1)
    forward(0, 2)
    forward(0, 3)
    forward(1, 1)
    forward(1, 2)
    forward(1, 3)
    forward(0, 2, True)
    forward(0, 3, True)
    forward(1, 1, True)
    forward(1, 2, True)
    forward(1, 3, True)
    relay_pack(0, 2)
    relay_pack(1, 2)
    prepare()
    order = [near[0], far[0], far[1], near[1]]
    stages = [[p] for p in order]
    pltpu.make_async_copy(w_buf, w_buf, w_sem).wait()
    back, waiting = None, []
    for stage in stages:
        for p in stage:
            arrived(p)
        fresh = [(p, multiplied(p)) for p in stage]
        for p, product in waiting:
            back = selected(p, product) if back is None else back + selected(p, product)
        if stage is not stages[-1] and back is not None:
            acc[...] = back
            back = acc[...]
        for p in stage:
            rows_copy(p).start()
        waiting = fresh
    for p, product in waiting:
        back = back + selected(p, product)
    shares = jnp.sum(hidden_buf[...] * back, axis=1, keepdims=True)
    share_buf[...] = jnp.broadcast_to(shares, (slots, 128)).astype(BF16).reshape(locals_, capacity, 128)
    for target in range(locals_):
        @pl.when(target != me_l)
        def _():
            remote(share_buf.at[target], back_buf.at[me_l], share_send, share_recv, {"local": target}).start()
    back_buf[me_l] = share_buf[me_l]
    scaled = state["weight"] * back
    ggate_out[...] = (scaled * gate_factor[...]).astype(BF16)
    gup_out[...] = (scaled * up_factor[...]).astype(BF16)
    mix_copy.wait_recv()
    for p in order:
        outer(p, p in (near[0], far[0]))

    sent(meta.at[0:nodes - 1], meta_send)
    sent(nraw.at[0:nodes - 1], raw_send)
    sent(zraw.at[0:locals_ - 1, 0], zraw_send)
    sent(zraw.at[:, 0:nodes - 1], plane_send)
    sent(cohort_meta.at[0:locals_ - 1], cmeta_send)
    pushed = relayed
    for d in range(1, locals_):
        for there in (me_l + d < locals_, me_l >= d):
            if d > REACH:
                there = there & (me_r == 0)
            pushed = pushed + there.astype(jnp.int32)
    for count in range(1, 2 * locals_):
        @pl.when(pushed == count)
        def _():
            for _ in range(count // locals_):
                sent(gath, pack_send)
            if count % locals_:
                sent(gath.at[0:count % locals_], pack_send)

    mix_copy.wait_send()
    sent(near_peer, rows_send.at[0])
    sent(far_peer, rows_send.at[1])
    sent(share_buf.at[0:locals_ - 1], share_send)
    chosen = [one_hot(hits[j], before[j:j + 1], capacity) for j in range(exp_group)]
    received(back_buf.at[0:locals_ - 1], share_recv)
    route = []
    for j in range(exp_group):
        value = jnp.zeros((capacity, 1), F32)
        for o in range(owners):
            value = value + back_buf[j * owners + o, :, 0:1].astype(F32)
        route.append(jnp.sum(chosen[j] * value, axis=0, keepdims=True))
    route_out[...] = stacked(route)[0:exp_group].astype(BF16)


def write_kernel(gate_in, up_in, down_in, route_in, gate_to, up_to, down_to, route_to, sems):
    pairs = ((down_in, down_to), (gate_in, gate_to), (up_in, up_to), (route_in, route_to))
    copies = [pltpu.make_async_copy(src, dst, sems.at[t]) for t, (src, dst) in enumerate(pairs)]
    for copy in copies:
        copy.start()
    for copy in copies:
        copy.wait()


def gathered(nodes, locals_, group_tok, grad_out, expert_ids, route_weights, gate_pre, up_pre, w_down_t):
    tok, width = grad_out.shape
    top = expert_ids.shape[1]
    slots, hs = gate_pre.shape
    owners = H // hs
    exp_group = locals_ // owners
    cohort = nodes * tok
    capacity = slots // locals_
    half = width // 2
    pairs, near_width, far_width = column_pairs(half)
    near_pairs = sum(1 for pair in pairs if pair[0] == "near")
    far_pairs = len(pairs) - near_pairs
    dims = (nodes, locals_, tok, top, width, hs, group_tok, owners)
    dma = pltpu.SemaphoreType.DMA
    hbm = pl.BlockSpec(memory_space=pltpu.HBM)
    shapes = (
        jax.ShapeDtypeStruct((slots, hs), BF16),
        jax.ShapeDtypeStruct((slots, hs), BF16),
        jax.ShapeDtypeStruct((half, hs), BF16),
        jax.ShapeDtypeStruct((exp_group, cohort), BF16),
    )
    results = pl.pallas_call(
        functools.partial(routed_kernel, dims),
        out_shape=shapes,
        in_specs=[hbm] * 6,
        out_specs=tuple([pl.BlockSpec(memory_space=pltpu.VMEM)] * 4),
        scratch_shapes=[
            pltpu.VMEM((2 * locals_ * (group_tok + cohort), hs), BF16),
            pltpu.VMEM((top, tok), jnp.int32),
            pltpu.VMEM((top, tok), BF16),
            pltpu.VMEM((nodes, 2 * top, tok), F32),
            pltpu.VMEM((locals_, exp_group, cohort), F32),
            pltpu.VMEM((nodes, tok, near_width), BF16),
            pltpu.VMEM((locals_, group_tok, near_width), BF16),
            pltpu.VMEM((locals_, nodes, tok, far_width), BF16),
            pltpu.VMEM((locals_ * cohort, far_width), BF16),
            pltpu.VMEM((locals_, group_tok, near_width // 2), BF16),
            pltpu.VMEM((locals_ * cohort, far_width // 2), BF16),
            pltpu.VMEM((width, hs), BF16),
            pltpu.VMEM((2, slots, hs), BF16),
            pltpu.VMEM((slots, hs), F32),
            pltpu.VMEM((slots, hs), F32),
            pltpu.VMEM((slots, hs), F32),
            pltpu.VMEM((slots, hs), F32),
            pltpu.VMEM((locals_, capacity, 128), BF16),
            pltpu.VMEM((locals_, capacity, 128), BF16),
            dma((4,)), dma(()), dma(()),
            dma(()), dma(()), dma(()), dma((near_pairs,)),
            dma(()), dma((locals_, far_pairs)), dma(()), dma((far_pairs,)), dma((far_pairs,)), dma((far_pairs,)),
            dma(()), dma((near_pairs,)), dma((max(1, locals_ - 1 - REACH), 2 if locals_ > 2 * REACH else 1, near_pairs)), dma(()), dma(()),
            dma(()), dma(()), dma((2,)), dma((2,)), dma(()), dma(()), pltpu.SemaphoreType.REGULAR,
        ],
        compiler_params=pltpu.CompilerParams(collective_id=0, has_side_effects=True, **KERNEL_PARAMS),
        name="routed",
    )(*[
        pltpu.with_memory_space_constraint(x, pltpu.HBM)
        for x in (expert_ids.T, route_weights.T, grad_out, gate_pre, up_pre, w_down_t)
    ])
    grad_gate, grad_up, grad_down, grad_route = pl.pallas_call(
        write_kernel,
        out_shape=shapes,
        in_specs=[pl.BlockSpec(memory_space=pl.ANY)] * 4,
        out_specs=tuple([pl.BlockSpec(memory_space=pl.ANY)] * 4),
        scratch_shapes=[dma((4,))],
        compiler_params=pltpu.CompilerParams(vmem_limit_bytes=1024 * 1024),
        name="write",
    )(*results)
    return grad_gate, grad_up, grad_down, grad_route.T


def swapped(block, axis, distance):
    count = lax.axis_size(axis)
    route = []
    for low in range(count):
        high = low | 1 << distance
        if high != low and high < count:
            route += [(low, high), (high, low)]
    return lax.ppermute(block, axis, route)


def outer_term(columns, weighted):
    return lax.dot_general(
        columns, weighted, (((0,), (0,)), ((), ())), preferred_element_type=jnp.float32
    )


def exchanged(grad_out, expert_ids, route_weights, gate_pre, up_pre, w_down_t):
    tok_dev, width = grad_out.shape
    slot_rows, hidden_slice = gate_pre.shape
    node_count = lax.axis_size("node")
    local_count = lax.axis_size("local")
    owners = H // hidden_slice
    exp_group = local_count // owners
    experts = exp_group * node_count
    capacity = slot_rows // local_count
    expert_range = lax.iota(jnp.int32, experts)
    route_hits = expert_ids[:, :, None] == expert_range[None, None, :]
    dense_weights = jnp.sum(
        jnp.where(route_hits, route_weights[:, :, None].astype(jnp.float32), 0.0), axis=1
    ).astype(jnp.bfloat16)
    cohort_grad, cohort_weights = (
        lax.all_gather(grad_out, "node", axis=0, tiled=True),
        lax.all_gather(dense_weights, "node", axis=0, tiled=True),
    )
    group_index = lax.axis_index("node")
    group_weights = lax.dynamic_slice_in_dim(cohort_weights, group_index * exp_group, exp_group, 1)
    routed = (group_weights != 0).astype(jnp.int32)
    position = lax.iota(jnp.int32, routed.shape[0])
    below = (position[:, None] > position[None, :]).astype(jnp.bfloat16)
    earlier = jnp.dot(below, routed.astype(jnp.bfloat16), preferred_element_type=jnp.float32).astype(jnp.int32)
    slot_range = lax.iota(jnp.int32, capacity)
    select = (routed[:, :, None] == 1) & (earlier[:, :, None] == slot_range[None, None, :])
    select_half = select.astype(jnp.bfloat16)
    packed = jnp.einsum(
        "cjs,cd->jsd", select_half, cohort_grad, preferred_element_type=jnp.float32
    ).astype(jnp.bfloat16)
    packed_weights = jnp.einsum(
        "cjs,cj->js", select_half, group_weights, preferred_element_type=jnp.float32
    ).astype(jnp.bfloat16)
    send_grad = jnp.broadcast_to(packed[:, None], (exp_group, owners, capacity, width)).reshape(
        local_count, capacity, width
    )
    send_weights = jnp.broadcast_to(packed_weights[:, None], (exp_group, owners, capacity)).reshape(
        local_count, capacity
    )
    recv_grad, recv_weights = (
        lax.all_to_all(send_grad, "local", split_axis=0, concat_axis=0, tiled=True),
        lax.all_to_all(send_weights, "local", split_axis=0, concat_axis=0, tiled=True),
    )
    cotangent = recv_grad.reshape(slot_rows, width)
    weight = recv_weights.reshape(slot_rows, 1).astype(jnp.float32)
    gate_value = gate_pre.astype(jnp.float32)
    up_value = up_pre.astype(jnp.float32)
    backward = jnp.dot(cotangent, w_down_t, preferred_element_type=jnp.float32)
    sigmoid_gate = jax.nn.sigmoid(gate_value)
    activated = gate_value * sigmoid_gate
    hidden = activated * up_value
    shares = jnp.sum(hidden * backward, axis=1).astype(jnp.bfloat16)
    scaled = weight * backward
    grad_gate_pre = (
        scaled * up_value * sigmoid_gate * (1.0 + gate_value * (1.0 - sigmoid_gate))
    ).astype(jnp.bfloat16)
    grad_up_pre = (scaled * activated).astype(jnp.bfloat16)
    weighted = (weight * hidden).astype(jnp.bfloat16)
    returned = lax.all_to_all(
        shares.reshape(local_count, capacity), "local", split_axis=0, concat_axis=0, tiled=True
    )
    slice_sum = jnp.sum(returned.astype(jnp.float32).reshape(exp_group, owners, capacity), axis=1)
    grad_route = jnp.sum(jnp.where(select, slice_sum[None], 0.0), axis=2).astype(jnp.bfloat16)
    half_width = width // lax.axis_size("rep")
    replica = lax.axis_index("rep")
    own_cols = lax.dynamic_slice_in_dim(cotangent, replica * half_width, half_width, 1)
    peer_cols = lax.dynamic_slice_in_dim(cotangent, (1 - replica) * half_width, half_width, 1)
    got_cols, got_weighted = swapped((peer_cols, weighted), "rep", 0)
    own_term = outer_term(own_cols, weighted).astype(jnp.bfloat16).astype(jnp.float32)
    peer_term = outer_term(got_cols, got_weighted).astype(jnp.bfloat16).astype(jnp.float32)
    grad_down_t = (own_term + peer_term).astype(jnp.bfloat16)
    return (grad_gate_pre, grad_up_pre, grad_down_t, grad_route)


def per_device(grad_out, expert_ids, route_weights, gate_pre, up_pre, w_down_t):
    nodes, locals_ = lax.axis_size("node"), lax.axis_size("local")
    capacity = gate_pre.shape[0] // locals_
    group_tok = grad_out.shape[0] * expert_ids.shape[1] // PER_GROUP
    args = (grad_out, expert_ids, route_weights, gate_pre, up_pre, w_down_t)
    if group_tok > capacity:
        return exchanged(*args)
    return gathered(nodes, locals_, group_tok, *args)


def solution(mesh):
    placed = (
        P(("node", "local", "rep"), None),
        P(("node", "local", "rep"), None),
        P(("node", "local", "rep"), None),
        P("rep", ("node", "local")),
        P("rep", ("node", "local")),
        P(None, ("node", "local")),
    )
    return jax.shard_map(
        per_device,
        mesh=mesh,
        in_specs=placed,
        out_specs=(
            P("rep", ("node", "local")),
            P("rep", ("node", "local")),
            P("rep", ("node", "local")),
            P(("local", "rep"), "node"),
        ),
        check_vma=False,
    )
```

```python
import functools
import jax
import jax.numpy as jnp
from jax import lax
from jax.experimental import pallas as pl
from jax.experimental.pallas import tpu as pltpu
from jax.sharding import PartitionSpec as P

H = 1024
PER_GROUP = 2
PAIRS = (("near", 4), ("far", 4), ("near", 4), ("far", 4))
TILE = 256
REACH = 2
MESH = pl.DeviceIdType.MESH
F32 = jnp.float32
BF16 = jnp.bfloat16
KERNEL_PARAMS = dict(vmem_limit_bytes=40 * 1024 * 1024)


def contract_rows(left, right):
    return lax.dot_general(left, right, (((0,), (0,)), ((), ())), preferred_element_type=F32)


def one_hot(member, row, height):
    places = lax.broadcasted_iota(jnp.int32, (height, member.shape[1]), 0).astype(F32)
    return jnp.where((member > 0) & (row == places), 1.0, 0.0)


def earlier_counts(rows, block):
    count = rows.shape[1]
    above = lax.broadcasted_iota(jnp.int32, (count, count), 0)
    col = lax.broadcasted_iota(jnp.int32, (count, count), 1)
    strict = jnp.where((above < col) & (above // block == col // block), 1.0, 0.0).astype(BF16)
    return jnp.dot(rows.astype(BF16), strict, preferred_element_type=F32)


def stacked(rows):
    lines = lax.broadcasted_iota(jnp.int32, (8, rows[0].shape[1]), 0)
    out = jnp.zeros(lines.shape, F32)
    for place, row in enumerate(rows):
        out = jnp.where(lines == place, row, out)
    return out


def column_pairs(half):
    parts = sum(share for _, share in PAIRS)
    pairs, taken, at = [], {"near": 0, "far": 0}, 0
    for way, share in PAIRS:
        size = half * share // parts
        pairs.append((way, at, size, taken[way]))
        taken[way] += 2 * size
        at += size
    return pairs, taken["near"], taken["far"]


def routed_kernel(
    dims, ids_ref, rw_ref, grad_ref, gate_ref, up_ref, w_ref,
    ggate_out, gup_out, down_out, route_out,
    mix, ids_buf, rw_buf, meta, cohort_meta, nraw, gath, zraw, far_rows, near_peer, far_peer, w_buf, gate_up,
    acc, hidden_buf, gate_factor, up_factor, share_buf, back_buf,
    own_sem, load_sem, w_sem,
    meta_send, meta_recv, raw_send, nraw_recv, zraw_send, zraw_recv, plane_send, plane_recv, hand_recv, own_recv,
    pack_send, pack_recv, relay_recv, cmeta_send, cmeta_recv,
    mix_send, mix_recv, rows_send, rows_recv, share_send, share_recv, turn,
):
    nodes, locals_, tok, top, width, hs, group_tok, owners = dims
    cohort = nodes * tok
    exp_group = locals_ // owners
    slots = gate_ref.shape[0]
    capacity = slots // locals_
    half = width // 2
    pairs, near_width, far_width = column_pairs(half)
    near = [p for p, pair in enumerate(pairs) if pair[0] == "near"]
    far = [p for p, pair in enumerate(pairs) if pair[0] == "far"]
    me_n, me_l, me_r = lax.axis_index("node"), lax.axis_index("local"), lax.axis_index("rep")
    peer = {"rep": 1 - me_r}

    def node_at(k):
        return {"node": lax.rem(me_n + k, nodes)}

    def local_at(k):
        return {"local": lax.rem(me_l + k, locals_)}

    def remote(src, dst, send, recv, device):
        return pltpu.make_async_remote_copy(
            src_ref=src, dst_ref=dst, send_sem=send, recv_sem=recv,
            device_id=device, device_id_type=MESH,
        )

    def received(ref, sem):
        remote(ref, ref, sem, sem, peer).wait_recv()

    def sent(ref, sem):
        remote(ref, ref, sem, sem, peer).wait_send()

    barrier = pltpu.get_barrier_semaphore()
    for k in range(1, nodes):
        pl.semaphore_signal(barrier, inc=1, device_id=node_at(k), device_id_type=MESH)
    for k in range(1, locals_):
        pl.semaphore_signal(barrier, inc=1, device_id=local_at(k), device_id_type=MESH)
    pl.semaphore_signal(barrier, inc=1, device_id=peer, device_id_type=MESH)

    def block(p):
        return pl.ds(pairs[p][3], 2 * pairs[p][2])

    def part(p):
        return pl.ds(pairs[p][1], pairs[p][2])

    id_copy = pltpu.make_async_copy(ids_ref, ids_buf, own_sem.at[0])
    rw_copy = pltpu.make_async_copy(rw_ref, rw_buf, own_sem.at[1])
    id_copy.start()
    rw_copy.start()
    for p, (way, at, size, place) in enumerate(pairs):
        for h in range(2):
            here = pl.ds(place + h * size, size)
            target = nraw.at[me_n, :, here] if way == "near" else zraw.at[me_l, me_n, :, here]
            pltpu.make_async_copy(
                grad_ref.at[:, pl.ds(h * half + at, size)], target, own_sem.at[2 if way == "near" else 3]
            ).start()
    pltpu.make_async_copy(gate_ref, gate_up.at[0], load_sem).start()
    pltpu.make_async_copy(up_ref, gate_up.at[1], load_sem).start()
    id_copy.wait()
    rw_copy.wait()
    meta[me_n, 0:top, :] = ids_buf[...].astype(F32)
    meta[me_n, top:2 * top, :] = rw_buf[...].astype(F32)
    own_near, own_far = nraw.at[me_n], zraw.at[me_l, me_n]
    pltpu.make_async_copy(own_near, own_near, own_sem.at[2]).wait()
    pltpu.make_async_copy(own_far, own_far, own_sem.at[3]).wait()
    pl.semaphore_wait(barrier, nodes + locals_ - 1)

    for k in range(1, nodes):
        remote(meta.at[me_n], meta.at[me_n], meta_send, meta_recv, node_at(k)).start()

    def beside(d):
        return [(me_l >= d, me_l - d), (me_l + d < locals_, me_l + d)]

    def far_block(l, n, p):
        return zraw.at[l, n, :, block(p)]

    for i, p in enumerate(near):
        for k in range(1, nodes):
            own = nraw.at[me_n, :, block(p)]
            remote(own, own, raw_send, nraw_recv.at[i], node_at(k)).start()
    for i, p in enumerate(far):
        for d in range(locals_ - 1, 0, -1):
            for there, target in beside(d):
                @pl.when(there)
                def _():
                    own = far_block(me_l, me_n, p)
                    remote(own, own, zraw_send, zraw_recv.at[me_l, i], {"local": target}).start()
    def spread(i, source, targets):
        piece = far_block(source, me_n, far[i])
        for target in targets:
            @pl.when(target != me_n)
            def _():
                remote(piece, piece, plane_send, plane_recv.at[i], {"node": target}).start()

    @pl.when(me_r == 1)
    def _():
        pl.semaphore_wait(turn, 1)

    square = nodes == 4
    beside_me = (me_n + 1 - 2 * lax.rem(me_n, 2), lax.rem(me_n + 2, 4))

    def hand(i):
        if square:
            piece = far_block(me_l, beside_me[i % 2], far[i])
            received(piece, hand_recv.at[i])
            remote(piece, piece, plane_send, own_recv.at[i], {"node": beside_me[1 - i % 2]}).start()

    for i in range(len(far)):
        own = far_block(me_l, me_n, far[i])
        if square:
            remote(own, own, plane_send, hand_recv.at[i], {"node": beside_me[i % 2]}).start()
            remote(own, own, plane_send, own_recv.at[i], {"node": beside_me[1 - i % 2]}).start()
        else:
            for k in range(1, nodes):
                remote(own, own, plane_send, own_recv.at[i], node_at(k)).start()

    @pl.when(me_r == 0)
    def _():
        pl.semaphore_signal(turn, inc=1, device_id=peer, device_id_type=MESH)

    w_at = 0
    w_rows = []
    for p, (way, at, size, place) in enumerate(pairs):
        for h in range(2):
            pltpu.make_async_copy(
                w_ref.at[pl.ds(h * half + at, size), :], w_buf.at[pl.ds(w_at + h * size, size), :], w_sem
            ).start()
        w_rows.append(pl.ds(w_at, 2 * size))
        w_at += 2 * size

    pltpu.make_async_copy(gate_up, gate_up, load_sem).wait()
    gate, up = gate_up[0].astype(F32), gate_up[1].astype(F32)
    sig = jax.nn.sigmoid(gate)
    act = gate * sig
    hidden_buf[...] = act * up
    up_factor[...] = act
    gate_factor[...] = up * sig * (1.0 + gate * (1.0 - sig))

    received(meta.at[0:nodes - 1], meta_recv)
    own_meta = jnp.concatenate([meta[n] for n in range(nodes)], axis=1)
    own_ids, own_rw = own_meta[0:top], own_meta[top:2 * top]
    low = (me_n * exp_group).astype(F32)
    named = [jnp.where(own_ids == low + j, 1.0, 0.0) for j in range(exp_group)]
    hits = [jnp.sum(match, axis=0, keepdims=True) for match in named]
    in_group = jnp.where(sum(hits) > 0, 1.0, 0.0)
    before = earlier_counts(stacked(hits + [in_group]), cohort)
    pick = one_hot(in_group, before[exp_group:exp_group + 1], group_tok).astype(BF16)

    def send_pack(i):
        p = near[i]
        received(nraw.at[0:nodes - 1, :, block(p)], nraw_recv.at[i])
        rows = nraw[:, :, block(p)].reshape(cohort, 2 * pairs[p][2])
        gath[me_l, :, block(p)] = jnp.dot(pick, rows, preferred_element_type=F32).astype(BF16)
        for d in range(locals_ - 1, 0, -1):
            for s, (there, target) in enumerate(((me_l + d < locals_, me_l + d), (me_l >= d, me_l - d))):
                if d > REACH:
                    there = there & (me_r == 0)
                send_to(i, d, s, there, me_l, target, d)

    sides = 2 if locals_ > 2 * REACH else 1

    def onward(d, s):
        return (me_r == 1) & ((me_l + d + 1 < locals_) if s == 0 else (me_l >= d + 1))

    def send_to(i, d, s, there, source, target, hop):
        pack = gath.at[source, :, block(near[i])]
        if REACH <= d < locals_ - 1:
            further = onward(hop, s)

            @pl.when(there & further)
            def _():
                remote(pack, pack, pack_send, relay_recv.at[d - REACH, s % sides, i], {"local": target}).start()

            there = there & jnp.logical_not(further)

        @pl.when(there)
        def _():
            remote(pack, pack, pack_send, pack_recv.at[i], {"local": target}).start()

    def send_cohort_meta():
        weights = [jnp.sum(match * own_rw, axis=0, keepdims=True) for match in named]
        cohort_meta[me_l] = stacked(weights)[0:exp_group]
        for k in range(1, locals_):
            own = cohort_meta.at[me_l]
            remote(own, own, cmeta_send, cmeta_recv, local_at(k)).start()

    def relays(d):
        return [
            ((me_r == 1) & (me_l >= d) & (me_l + 1 < locals_), me_l - d, me_l + 1),
            ((me_r == 1) & (me_l + d < locals_) & (me_l >= 1), me_l + d, me_l - 1),
        ]

    def relay_pack(i, d):
        for s, (there, source, target) in enumerate(relays(d)):
            @pl.when(there)
            def _():
                received(gath.at[source, :, block(near[i])], relay_recv.at[d - REACH, s % sides, i])

            send_to(i, d + 1, s, there, source, target, 1)

    def forward(i, d, rest=False):
        for there, source in beside(d):
            @pl.when(there)
            def _():
                if not rest:
                    received(far_block(source, me_n, far[i]), zraw_recv.at[source, i])
                spread(i, source, range(1, nodes) if rest else range(1))

    state = {}

    def prepare():
        received(cohort_meta.at[0:locals_ - 1], cmeta_recv)
        total = locals_ * cohort
        weights = jnp.concatenate([cohort_meta[l] for l in range(locals_)], axis=1)
        mine = lax.broadcasted_iota(jnp.int32, (exp_group, total), 0) == me_l // owners
        row_weight = jnp.sum(jnp.where(mine, weights, 0.0), axis=0, keepdims=True)
        member = jnp.where(row_weight > 0, 1.0, 0.0)
        grouped = jnp.where(jnp.sum(weights, axis=0, keepdims=True) > 0, 1.0, 0.0)
        earlier = earlier_counts(stacked([member, grouped]), cohort)
        which = (lax.broadcasted_iota(jnp.int32, (1, total), 1) // cohort).astype(F32)
        slot_hot = one_hot(member, earlier[0:1] + which * capacity, slots)
        pack_hot = one_hot(grouped, earlier[1:2] + which * group_tok, locals_ * group_tok)
        state["far"] = slot_hot.astype(BF16)
        state["near"] = lax.dot_general(
            slot_hot.astype(BF16), pack_hot.astype(BF16),
            (((1,), (1,)), ((), ())), preferred_element_type=F32,
        ).astype(BF16)
        weight = jnp.sum(slot_hot * row_weight, axis=1, keepdims=True)
        state["weight"] = weight
        weighted = (weight * hidden_buf[...]).astype(BF16)
        for way in ways:
            mix[mix_rows(way, 0), :] = contract_rows(state[way], weighted).astype(BF16)
        mix_copy.start()

    ways = ("near", "far")
    mix_half = mix.shape[0] // 2
    mix_copy = remote(mix.at[0:mix_half, :], mix.at[mix_half:2 * mix_half, :], mix_send, mix_recv, peer)

    def mix_rows(way, r):
        start = 0 if way == "near" else locals_ * group_tok
        return pl.ds(r * mix_half + start, locals_ * (group_tok if way == "near" else cohort))

    def half_of(p, r):
        return pl.ds(pl.multiple_of(pairs[p][3] + r * pairs[p][2], 128), pairs[p][2])

    def peer_part(p):
        return pl.ds(pairs[p][3] // 2, pairs[p][2])

    def rows_copy(p):
        w, there = ways.index(pairs[p][0]), half_of(p, 1 - me_r)
        if w == 0:
            return remote(gath.at[:, :, there], near_peer.at[:, :, peer_part(p)], rows_send.at[w], rows_recv.at[w], peer)
        return remote(far_rows.at[:, there], far_peer.at[:, peer_part(p)], rows_send.at[w], rows_recv.at[w], peer)

    relayed = sum(there.astype(jnp.int32) for d in range(REACH, locals_ - 1) for there, _, _ in relays(d))

    def arrived(p):
        if pairs[p][0] == "far":
            i = far.index(p)
            received(zraw.at[me_l, 0:nodes - 1 - square, :, block(p)], own_recv.at[i])
            received(zraw.at[0:locals_ - 1, 0:nodes - 1, :, block(p)], plane_recv.at[i])
            return
        for count in range(1, locals_):
            @pl.when(locals_ - 1 - relayed == count)
            def _():
                received(gath.at[0:count, :, block(p)], pack_recv.at[near.index(p)])

    def multiplied(p):
        way, at, size, place = pairs[p]
        if way == "far":
            rows = zraw[:, :, :, block(p)].reshape(locals_ * cohort, 2 * size)
            far_rows[:, block(p)] = rows
        else:
            rows = gath[:, :, block(p)].reshape(locals_ * group_tok, 2 * size)
        return jnp.dot(rows, w_buf[w_rows[p], :], preferred_element_type=F32).astype(BF16)

    def selected(p, product):
        return jnp.dot(state[pairs[p][0]], product, preferred_element_type=F32)

    def outer(p, fresh):
        way, at, size, place = pairs[p]
        if fresh:
            received(near_peer if way == "near" else far_peer, rows_recv.at[ways.index(way)])
        for t in range(0, size, TILE):
            wide = min(TILE, size - t)
            mine = pl.ds(pl.multiple_of(place + me_r * size + t, 128), wide)
            theirs = pl.ds(place // 2 + t, wide)
            if way == "near":
                pieces = [
                    gath[:, :, mine].reshape(locals_ * group_tok, wide),
                    near_peer[:, :, theirs].reshape(locals_ * group_tok, wide),
                ]
            else:
                pieces = [far_rows[:, mine], far_peer[:, theirs]]
            down_out[pl.ds(at + t, wide), :] = contract_rows(
                jnp.concatenate(pieces, axis=0),
                jnp.concatenate([mix[mix_rows(way, 0), :], mix[mix_rows(way, 1), :]], axis=0),
            ).astype(BF16)

    send_cohort_meta()
    send_pack(0)
    forward(0, 1)
    forward(0, 1, True)
    hand(0)
    send_pack(1)
    hand(1)
    forward(0, 2)
    forward(0, 3)
    forward(1, 1)
    forward(1, 2)
    forward(1, 3)
    forward(0, 2, True)
    forward(0, 3, True)
    forward(1, 1, True)
    forward(1, 2, True)
    forward(1, 3, True)
    relay_pack(0, 2)
    relay_pack(1, 2)
    prepare()
    order = [near[0], far[0], far[1], near[1]]
    stages = [[p] for p in order]
    pltpu.make_async_copy(w_buf, w_buf, w_sem).wait()
    back, waiting = None, []
    for stage in stages:
        for p in stage:
            arrived(p)
        fresh = [(p, multiplied(p)) for p in stage]
        for p, product in waiting:
            back = selected(p, product) if back is None else back + selected(p, product)
        if stage is not stages[-1] and back is not None:
            acc[...] = back
            back = acc[...]
        for p in stage:
            rows_copy(p).start()
        waiting = fresh
    for p, product in waiting:
        back = back + selected(p, product)
    shares = jnp.sum(hidden_buf[...] * back, axis=1, keepdims=True)
    share_buf[...] = jnp.broadcast_to(shares, (slots, 128)).astype(BF16).reshape(locals_, capacity, 128)
    for target in range(locals_):
        @pl.when(target != me_l)
        def _():
            remote(share_buf.at[target], back_buf.at[me_l], share_send, share_recv, {"local": target}).start()
    back_buf[me_l] = share_buf[me_l]
    scaled = state["weight"] * back
    ggate_out[...] = (scaled * gate_factor[...]).astype(BF16)
    gup_out[...] = (scaled * up_factor[...]).astype(BF16)
    mix_copy.wait_recv()
    for p in order:
        outer(p, p in (near[0], far[0]))

    sent(meta.at[0:nodes - 1], meta_send)
    sent(nraw.at[0:nodes - 1], raw_send)
    sent(zraw.at[0:locals_ - 1, 0], zraw_send)
    sent(zraw.at[:, 0:nodes - 1], plane_send)
    sent(cohort_meta.at[0:locals_ - 1], cmeta_send)
    pushed = relayed
    for d in range(1, locals_):
        for there in (me_l + d < locals_, me_l >= d):
            if d > REACH:
                there = there & (me_r == 0)
            pushed = pushed + there.astype(jnp.int32)
    for count in range(1, 2 * locals_):
        @pl.when(pushed == count)
        def _():
            for _ in range(count // locals_):
                sent(gath, pack_send)
            if count % locals_:
                sent(gath.at[0:count % locals_], pack_send)

    mix_copy.wait_send()
    sent(near_peer, rows_send.at[0])
    sent(far_peer, rows_send.at[1])
    sent(share_buf.at[0:locals_ - 1], share_send)
    chosen = [one_hot(hits[j], before[j:j + 1], capacity) for j in range(exp_group)]
    received(back_buf.at[0:locals_ - 1], share_recv)
    route = []
    for j in range(exp_group):
        value = jnp.zeros((capacity, 1), F32)
        for o in range(owners):
            value = value + back_buf[j * owners + o, :, 0:1].astype(F32)
        route.append(jnp.sum(chosen[j] * value, axis=0, keepdims=True))
    route_out[...] = stacked(route)[0:exp_group].astype(BF16)


def write_kernel(gate_in, up_in, down_in, route_in, gate_to, up_to, down_to, route_to, sems):
    pairs = ((down_in, down_to), (gate_in, gate_to), (up_in, up_to), (route_in, route_to))
    copies = [pltpu.make_async_copy(src, dst, sems.at[t]) for t, (src, dst) in enumerate(pairs)]
    for copy in copies:
        copy.start()
    for copy in copies:
        copy.wait()


def gathered(nodes, locals_, group_tok, grad_out, expert_ids, route_weights, gate_pre, up_pre, w_down_t):
    tok, width = grad_out.shape
    top = expert_ids.shape[1]
    slots, hs = gate_pre.shape
    owners = H // hs
    exp_group = locals_ // owners
    cohort = nodes * tok
    capacity = slots // locals_
    half = width // 2
    pairs, near_width, far_width = column_pairs(half)
    near_pairs = sum(1 for pair in pairs if pair[0] == "near")
    far_pairs = len(pairs) - near_pairs
    dims = (nodes, locals_, tok, top, width, hs, group_tok, owners)
    dma = pltpu.SemaphoreType.DMA
    hbm = pl.BlockSpec(memory_space=pltpu.HBM)
    shapes = (
        jax.ShapeDtypeStruct((slots, hs), BF16),
        jax.ShapeDtypeStruct((slots, hs), BF16),
        jax.ShapeDtypeStruct((half, hs), BF16),
        jax.ShapeDtypeStruct((exp_group, cohort), BF16),
    )
    results = pl.pallas_call(
        functools.partial(routed_kernel, dims),
        out_shape=shapes,
        in_specs=[hbm] * 6,
        out_specs=tuple([pl.BlockSpec(memory_space=pltpu.VMEM)] * 4),
        scratch_shapes=[
            pltpu.VMEM((2 * locals_ * (group_tok + cohort), hs), BF16),
            pltpu.VMEM((top, tok), jnp.int32),
            pltpu.VMEM((top, tok), BF16),
            pltpu.VMEM((nodes, 2 * top, tok), F32),
            pltpu.VMEM((locals_, exp_group, cohort), F32),
            pltpu.VMEM((nodes, tok, near_width), BF16),
            pltpu.VMEM((locals_, group_tok, near_width), BF16),
            pltpu.VMEM((locals_, nodes, tok, far_width), BF16),
            pltpu.VMEM((locals_ * cohort, far_width), BF16),
            pltpu.VMEM((locals_, group_tok, near_width // 2), BF16),
            pltpu.VMEM((locals_ * cohort, far_width // 2), BF16),
            pltpu.VMEM((width, hs), BF16),
            pltpu.VMEM((2, slots, hs), BF16),
            pltpu.VMEM((slots, hs), F32),
            pltpu.VMEM((slots, hs), F32),
            pltpu.VMEM((slots, hs), F32),
            pltpu.VMEM((slots, hs), F32),
            pltpu.VMEM((locals_, capacity, 128), BF16),
            pltpu.VMEM((locals_, capacity, 128), BF16),
            dma((4,)), dma(()), dma(()),
            dma(()), dma(()), dma(()), dma((near_pairs,)),
            dma(()), dma((locals_, far_pairs)), dma(()), dma((far_pairs,)), dma((far_pairs,)), dma((far_pairs,)),
            dma(()), dma((near_pairs,)), dma((max(1, locals_ - 1 - REACH), 2 if locals_ > 2 * REACH else 1, near_pairs)), dma(()), dma(()),
            dma(()), dma(()), dma((2,)), dma((2,)), dma(()), dma(()), pltpu.SemaphoreType.REGULAR,
        ],
        compiler_params=pltpu.CompilerParams(collective_id=0, has_side_effects=True, **KERNEL_PARAMS),
        name="routed",
    )(*[
        pltpu.with_memory_space_constraint(x, pltpu.HBM)
        for x in (expert_ids.T, route_weights.T, grad_out, gate_pre, up_pre, w_down_t)
    ])
    grad_gate, grad_up, grad_down, grad_route = pl.pallas_call(
        write_kernel,
        out_shape=shapes,
        in_specs=[pl.BlockSpec(memory_space=pl.ANY)] * 4,
        out_specs=tuple([pl.BlockSpec(memory_space=pl.ANY)] * 4),
        scratch_shapes=[dma((4,))],
        compiler_params=pltpu.CompilerParams(vmem_limit_bytes=1024 * 1024),
        name="write",
    )(*results)
    return grad_gate, grad_up, grad_down, grad_route.T


def swapped(block, axis, distance):
    count = lax.axis_size(axis)
    route = []
    for low in range(count):
        high = low | 1 << distance
        if high != low and high < count:
            route += [(low, high), (high, low)]
    return lax.ppermute(block, axis, route)


def outer_term(columns, weighted):
    return lax.dot_general(
        columns, weighted, (((0,), (0,)), ((), ())), preferred_element_type=jnp.float32
    )


def exchanged(grad_out, expert_ids, route_weights, gate_pre, up_pre, w_down_t):
    tok_dev, width = grad_out.shape
    slot_rows, hidden_slice = gate_pre.shape
    node_count = lax.axis_size("node")
    local_count = lax.axis_size("local")
    owners = H // hidden_slice
    exp_group = local_count // owners
    experts = exp_group * node_count
    capacity = slot_rows // local_count
    expert_range = lax.iota(jnp.int32, experts)
    route_hits = expert_ids[:, :, None] == expert_range[None, None, :]
    dense_weights = jnp.sum(
        jnp.where(route_hits, route_weights[:, :, None].astype(jnp.float32), 0.0), axis=1
    ).astype(jnp.bfloat16)
    cohort_grad, cohort_weights = (
        lax.all_gather(grad_out, "node", axis=0, tiled=True),
        lax.all_gather(dense_weights, "node", axis=0, tiled=True),
    )
    group_index = lax.axis_index("node")
    group_weights = lax.dynamic_slice_in_dim(cohort_weights, group_index * exp_group, exp_group, 1)
    routed = (group_weights != 0).astype(jnp.int32)
    position = lax.iota(jnp.int32, routed.shape[0])
    below = (position[:, None] > position[None, :]).astype(jnp.bfloat16)
    earlier = jnp.dot(below, routed.astype(jnp.bfloat16), preferred_element_type=jnp.float32).astype(jnp.int32)
    slot_range = lax.iota(jnp.int32, capacity)
    select = (routed[:, :, None] == 1) & (earlier[:, :, None] == slot_range[None, None, :])
    select_half = select.astype(jnp.bfloat16)
    packed = jnp.einsum(
        "cjs,cd->jsd", select_half, cohort_grad, preferred_element_type=jnp.float32
    ).astype(jnp.bfloat16)
    packed_weights = jnp.einsum(
        "cjs,cj->js", select_half, group_weights, preferred_element_type=jnp.float32
    ).astype(jnp.bfloat16)
    send_grad = jnp.broadcast_to(packed[:, None], (exp_group, owners, capacity, width)).reshape(
        local_count, capacity, width
    )
    send_weights = jnp.broadcast_to(packed_weights[:, None], (exp_group, owners, capacity)).reshape(
        local_count, capacity
    )
    recv_grad, recv_weights = (
        lax.all_to_all(send_grad, "local", split_axis=0, concat_axis=0, tiled=True),
        lax.all_to_all(send_weights, "local", split_axis=0, concat_axis=0, tiled=True),
    )
    cotangent = recv_grad.reshape(slot_rows, width)
    weight = recv_weights.reshape(slot_rows, 1).astype(jnp.float32)
    gate_value = gate_pre.astype(jnp.float32)
    up_value = up_pre.astype(jnp.float32)
    backward = jnp.dot(cotangent, w_down_t, preferred_element_type=jnp.float32)
    sigmoid_gate = jax.nn.sigmoid(gate_value)
    activated = gate_value * sigmoid_gate
    hidden = activated * up_value
    shares = jnp.sum(hidden * backward, axis=1).astype(jnp.bfloat16)
    scaled = weight * backward
    grad_gate_pre = (
        scaled * up_value * sigmoid_gate * (1.0 + gate_value * (1.0 - sigmoid_gate))
    ).astype(jnp.bfloat16)
    grad_up_pre = (scaled * activated).astype(jnp.bfloat16)
    weighted = (weight * hidden).astype(jnp.bfloat16)
    returned = lax.all_to_all(
        shares.reshape(local_count, capacity), "local", split_axis=0, concat_axis=0, tiled=True
    )
    slice_sum = jnp.sum(returned.astype(jnp.float32).reshape(exp_group, owners, capacity), axis=1)
    grad_route = jnp.sum(jnp.where(select, slice_sum[None], 0.0), axis=2).astype(jnp.bfloat16)
    half_width = width // lax.axis_size("rep")
    replica = lax.axis_index("rep")
    own_cols = lax.dynamic_slice_in_dim(cotangent, replica * half_width, half_width, 1)
    peer_cols = lax.dynamic_slice_in_dim(cotangent, (1 - replica) * half_width, half_width, 1)
    got_cols, got_weighted = swapped((peer_cols, weighted), "rep", 0)
    own_term = outer_term(own_cols, weighted).astype(jnp.bfloat16).astype(jnp.float32)
    peer_term = outer_term(got_cols, got_weighted).astype(jnp.bfloat16).astype(jnp.float32)
    grad_down_t = (own_term + peer_term).astype(jnp.bfloat16)
    return (grad_gate_pre, grad_up_pre, grad_down_t, grad_route)


def per_device(grad_out, expert_ids, route_weights, gate_pre, up_pre, w_down_t):
    nodes, locals_ = lax.axis_size("node"), lax.axis_size("local")
    capacity = gate_pre.shape[0] // locals_
    group_tok = grad_out.shape[0] * expert_ids.shape[1] // PER_GROUP
    args = (grad_out, expert_ids, route_weights, gate_pre, up_pre, w_down_t)
    if group_tok > capacity:
        return exchanged(*args)
    return gathered(nodes, locals_, group_tok, *args)


def solution(mesh):
    placed = (
        P(("node", "local", "rep"), None),
        P(("node", "local", "rep"), None),
        P(("node", "local", "rep"), None),
        P("rep", ("node", "local")),
        P("rep", ("node", "local")),
        P(None, ("node", "local")),
    )
    return jax.shard_map(
        per_device,
        mesh=mesh,
        in_specs=placed,
        out_specs=(
            P("rep", ("node", "local")),
            P("rep", ("node", "local")),
            P("rep", ("node", "local")),
            P(("local", "rep"), "node"),
        ),
        check_vma=False,
    )
```
